32 devices in a mesh: rep: 4 (over y, x), fsdp: 2 (over core), tp: 4 (over z).
Axes of the slice: x: 2, y: 2, z: 4, core: 2. Of those that a mesh axis runs over, the one named last changes fastest.
Arguments:
- grad_parts: bfloat16 [2, 2, 8192, 1024], P('fsdp', None, 'rep', 'tp'), may hold values from -4 to 4
- master_weight: float32 [2, 8192, 1024], P(None, ('rep', 'fsdp'), 'tp'), may hold values from -0.0625 to 0.0625
- moment_one: float32 [2, 8192, 1024], P(None, ('rep', 'fsdp'), 'tp'), may hold values from -4 to 4
- moment_two: float32 [2, 8192, 1024], P(None, ('rep', 'fsdp'), 'tp'), may hold values from 0.1 to 2
- layer_inputs: bfloat16 [384, 4, 8192], P(('rep', 'fsdp'), None, 'tp'), may hold values from -6 to 6
- queries: bfloat16 [384, 4, 8192], P(('rep', 'fsdp'), None, 'tp'), may hold values from -105 to 105
- kv_cache: bfloat16 [384, 24, 2, 1024], P(('rep', 'fsdp'), None, None, 'tp'), may hold values from -4 to 4
- lengths: int32 [384], P(('rep', 'fsdp')), may hold values from 2 to 24
Outputs:
- new_master: float32 [2, 8192, 1024], P(None, ('rep', 'fsdp'), 'tp')
- new_moment_one: float32 [2, 8192, 1024], P(None, ('rep', 'fsdp'), 'tp')
- new_moment_two: float32 [2, 8192, 1024], P(None, ('rep', 'fsdp'), 'tp')
- context: bfloat16 [384, 4, 8192], P(('rep', 'fsdp'), None, 'tp')
The draws below stay inside these ranges and needn't reach their ends.
Inputs may be any that keep to these rules, and one draw needn't show every extreme that they name: lengths[r] is the number of valid cached positions of row r, at most 24.
All inputs are finite; a program needn't handle non-finite values.
Results may differ from the reference program's by a relative error of at most 0.0065.
Values may be sent and summed in bfloat16 or wider, within the bound.
A program may use at most 64 MiB of HBM per device.

```python
import math
import jax
import jax.numpy as jnp
from jax import lax

D = 8192
QH = 64
KVH = 8
HD = 128
ROW_DEV = 48
CACHE = 24
STEPS = 4
ROWS = 384
KVW = 1024
N_FSDP = 2


def shared_cache(key):
    base = jax.random.normal(jax.random.fold_in(key, 11), (ROWS, CACHE, 2, KVH * HD), jnp.float32)
    base = jnp.clip(base, -4.0, 4.0)
    return base


def draw_kv_cache(key, part):
    return shared_cache(key).astype(jnp.bfloat16)


def draw_queries(key, part):
    drawn = jax.random.normal(jax.random.fold_in(key, 12), (ROWS, STEPS, QH * HD), jnp.float32)
    drawn = jnp.clip(drawn, -4.0, 4.0)
    return drawn.astype(jnp.bfloat16)


def set_ends(array, key, smallest, top_value):
    extent = array.shape
    index_at = [jax.random.randint(jax.random.fold_in(key, axis), (), 0, extent[axis]) for axis in range(len(extent))]
    array = array.at[tuple(index_at)].set(smallest)
    longest = extent.index(max(extent))
    index_at[longest] = (index_at[longest] + 1) % extent[longest]
    return array.at[tuple(index_at)].set(top_value)


def spiked(drawn, stream_key, source, target, shards_of, factor):
    owner, partner = [(jnp.arange(drawn.shape[position]) // (drawn.shape[position] // shards_of)).reshape([-1 if axis == position else 1 for axis in range(drawn.ndim)]) for position in (source, target)]
    chosen = jax.random.permutation(stream_key, shards_of)[partner]
    strong = (owner == chosen) | (owner == (partner + shards_of // 2) % shards_of)
    return jnp.where(strong, factor * drawn, drawn)


def block_scale(stream_key, dims, split, smallest, largest):
    gain, own = 1.0, jax.random.fold_in(stream_key, 6)
    for position, blocks in split:
        steps = jnp.exp(jax.random.uniform(jax.random.fold_in(own, position), (blocks,), jnp.float32, smallest / len(split), largest / len(split)))
        gain = gain * jnp.repeat(steps, dims[position] // blocks).reshape([-1 if axis == position else 1 for axis in range(len(dims))])
    return gain


def noise(key, shape, spread, bound, cuts=(), held_as=jnp.bfloat16):
    gain = block_scale(key, shape, cuts, -0.22, 0.18) if cuts else 1.0
    array = jax.random.normal(key, shape, jnp.float32) * spread * gain
    return jnp.minimum(jnp.maximum(array, -bound), bound).astype(held_as)


def bell_draw_with(key, dims, spread, most, cuts, heavy, kind=jnp.bfloat16):
    values = spread * jax.random.normal(key, dims, jnp.float32)
    if cuts:
        values = values * block_scale(key, dims, cuts, -0.22, 0.18)
    return jnp.clip(spiked(values, jax.random.fold_in(key, 3), *heavy), -most, most).astype(kind)


def setup_inputs(seed: int = 0) -> dict:
    splits = jax.random.split(jax.random.key(seed), 9)
    grad_parts = bell_draw_with(splits[0], (N_FSDP, 2, D, KVW), 0.5, 4.0, ((0, 2), (2, 4), (3, 4)), (0, 2, 2, 2.0))
    master_weight = noise(splits[1], (2, D, KVW), D ** -0.5, 0.0625, ((1, 8), (2, 4)), jnp.float32)
    moment_one = noise(splits[2], (2, D, KVW), 0.3, 4.0, ((1, 8), (2, 4)), jnp.float32)
    moment_two = jnp.clip(jnp.exp(math.log(2.0) - 2.9957323 * jax.random.uniform(splits[3], (2, D, KVW), jnp.float32) ** block_scale(splits[3], (2, D, KVW), ((1, 8), (2, 4)), -0.2, 0.2)), 0.1, 2.0)
    layer_inputs = noise(splits[4], (ROWS, STEPS, D), 1.0, 6.0, ((0, 8), (2, 4)))
    queries = draw_queries(jax.random.fold_in(splits[8], 71), 0)
    kv_cache = draw_kv_cache(jax.random.fold_in(splits[8], 71), 0)
    lengths = set_ends(jax.random.randint(splits[7], (ROWS,), 2, CACHE + 1), jax.random.fold_in(splits[7], 1), 2, CACHE).astype(jnp.int32)
    return {"grad_parts": grad_parts, "master_weight": master_weight, "moment_one": moment_one, "moment_two": moment_two, "layer_inputs": layer_inputs, "queries": queries, "kv_cache": kv_cache, "lengths": lengths}


beta_one = 0.9
beta_two = 0.95
learning_rate = 0.001
weight_decay = 0.1
epsilon = 1e-08
first_bias = 1.0 - 0.9 ** 10
second_bias = 1.0 - 0.95 ** 10

def adamw_update(gradient, master, moment_one, moment_two):
    new_one = beta_one * moment_one + (1.0 - beta_one) * gradient
    new_two = beta_two * moment_two + (1.0 - beta_two) * gradient * gradient
    update = new_one / first_bias / (jnp.sqrt(new_two / second_bias) + epsilon)
    new_master = master - learning_rate * (update + weight_decay * master)
    return (new_one, new_two, new_master)

def attend(pieces):
    query_block, cache_block, fresh_keys, fresh_values, length_block = pieces
    row_count = query_block.shape[0]
    step_count = query_block.shape[1]
    kv_heads = fresh_keys.shape[2]
    cache_len = cache_block.shape[1]
    grouped = query_block.reshape(row_count, step_count, kv_heads, -1, HD).astype(jnp.float32)
    cached_keys = cache_block[:, :, 0].reshape(row_count, cache_len, kv_heads, HD).astype(jnp.float32)
    cached_values = cache_block[:, :, 1].reshape(row_count, cache_len, kv_heads, HD).astype(jnp.float32)
    scaling = 1.0 / jnp.sqrt(jnp.float32(HD))
    cached_scores = jnp.einsum('rsgqd,rcgd->rsgqc', grouped, cached_keys) * scaling
    fresh_scores = jnp.einsum('rsgqd,rugd->rsgqu', grouped, fresh_keys.astype(jnp.float32)) * scaling
    valid_old = jnp.arange(cache_len, dtype=jnp.int32)[None, :] < length_block[:, None]
    valid_old = valid_old[:, None, None, None, :]
    steps_index = jnp.arange(step_count, dtype=jnp.int32)
    valid_new = (steps_index[None, :] <= steps_index[:, None])[None, :, None, None, :]
    scores = jnp.concatenate([jnp.where(valid_old, cached_scores, -jnp.inf), jnp.where(valid_new, fresh_scores, -jnp.inf)], axis=-1)
    row_max = lax.optimization_barrier(jnp.max(scores, axis=-1, keepdims=True))
    exponent = jnp.exp(scores - row_max)
    weights = (exponent / lax.optimization_barrier(jnp.sum(exponent, axis=-1, keepdims=True))).astype(jnp.bfloat16).astype(jnp.float32)
    output = jnp.einsum('rsgqc,rcgd->rsgqd', weights[..., :cache_len], cached_values)
    output = output + jnp.einsum('rsgqu,rugd->rsgqd', weights[..., cache_len:], fresh_values.astype(jnp.float32))
    return output.astype(jnp.bfloat16).reshape(row_count, step_count, -1)

def reference(grad_parts, master_weight, moment_one, moment_two, layer_inputs, queries, kv_cache, lengths):
    gradient = lax.optimization_barrier(jnp.sum(grad_parts.astype(jnp.float32), axis=0))
    new_one, new_two, new_master = adamw_update(gradient, master_weight, moment_one, moment_two)
    rollout_weight = new_master.astype(jnp.bfloat16)
    flattened = layer_inputs.reshape(ROWS * STEPS, D)
    fresh_keys = jnp.dot(flattened, rollout_weight[0], preferred_element_type=jnp.float32).astype(jnp.bfloat16)
    fresh_values = jnp.dot(flattened, rollout_weight[1], preferred_element_type=jnp.float32).astype(jnp.bfloat16)
    blocks = ROWS // ROW_DEV
    pieces = (queries.reshape(blocks, ROW_DEV, STEPS, QH * HD), kv_cache.reshape(blocks, ROW_DEV, CACHE, 2, KVH * HD), fresh_keys.reshape(blocks, ROW_DEV, STEPS, KVH, HD), fresh_values.reshape(blocks, ROW_DEV, STEPS, KVH, HD), lengths.reshape(blocks, ROW_DEV))
    context = lax.map(attend, pieces).reshape(ROWS, STEPS, QH * HD)
    return (new_master, new_one, new_two, context)
```

```python
import functools

import jax
import jax.numpy as jnp
from jax import lax
from jax.experimental import pallas as pl
from jax.experimental.pallas import tpu as pltpu
from jax.sharding import PartitionSpec as P

HD = 128
MESH = pl.DeviceIdType.MESH
W_CHUNKS = 2
GROUPS = 4
ADAM_SUB = 32
TAIL_ROWS = 8
TAIL_BLOCKS = 3
LOG2E = 1.4426950408889634


def learner_kernel(
    grad_hbm, master_hbm, one_hbm, two_hbm, x_hbm, kv_hbm,
    fresh_out, cached_out, master_out, one_out, two_out,
    own_grad, peer_grad, master, one, two, wpair, wbuf, xbuf, xflat,
    far, far_peer, far_out, far_in, near, near_peer, kv_raw, kv_flat,
    grad_sem, state_sem, x_sem, kv_sem, out_sem, grad_send, grad_recv, x_send, x_recv,
    pair_send, pair_recv, w_send, w_recv, w_fwd_send, far_send, far_recv, back_send, back_recv, near_send, near_recv,
):
    r, f, t = lax.axis_index("rep"), lax.axis_index("fsdp"), lax.axis_index("tp")
    nf = 1 - f
    rx = r + 1 - 2 * lax.rem(r, 2)
    ry = lax.rem(r + 2, 4)
    rd = lax.rem(rx + 2, 4)
    partner, dev_x, dev_y = (r, nf, t), (rx, f, t), (ry, f, t)
    pair = t + 1 - 2 * lax.rem(t, 2)
    mirror = 3 - t
    pair_mirror = 3 - pair
    middle = (t == 1) | (t == 2)
    mine = lax.rem((t + 1) // 2, 2)
    theirs = 1 - mine
    depth = master.shape[1]
    half = depth // 2
    chunk = half // W_CHUNKS
    x_rows, x_steps = xbuf.shape[2:4]
    group_rows = x_rows // GROUPS
    group_tokens = group_rows * x_steps
    blocks = wbuf.shape[2] // half

    def state_rows(sub, c):
        return pl.ds(pl.multiple_of(sub * half + c * chunk, chunk), chunk)

    def owner_rows(owner, c):
        return pl.ds(pl.multiple_of(owner * half + c * chunk, chunk), chunk)

    order = []
    for c in range(W_CHUNKS):
        order += [(theirs, c), (mine, c)]

    def features(h, sub):
        return pl.ds(pl.multiple_of(h * depth + sub * half, half), half)

    def some_rows(g):
        return pl.ds(g * group_rows, group_rows)

    def tokens(g):
        return pl.ds(pl.multiple_of(g * group_tokens, group_tokens), group_tokens)

    grad_local, state_local = [], []
    for i, (sub, c) in enumerate(order):
        at = state_rows(sub, c)
        source = pl.ds(pl.multiple_of(f * depth + sub * half + c * chunk, chunk), chunk)
        grad_local.append(
            pltpu.make_async_copy(grad_hbm.at[0, :, source, :], own_grad.at[:, at, :], grad_sem.at[i])
        )
        state_local.append([
            pltpu.make_async_copy(hbm.at[:, at, :], vmem.at[:, at, :], state_sem.at[j, i])
            for j, (hbm, vmem) in enumerate(((master_hbm, master), (one_hbm, one), (two_hbm, two)))
        ])
        grad_local[i].start()
        for copy in state_local[i]:
            copy.start()
    x_local = pltpu.make_async_copy(x_hbm.at[:, :, features(f, mine)], xbuf.at[t, f], x_sem.at[0])
    kv_local = pltpu.make_async_copy(kv_hbm, kv_raw, kv_sem.at[0])
    x_local.start()
    kv_local.start()

    barrier = pltpu.get_barrier_semaphore()
    friends = [partner, dev_x, dev_y]
    for i in range(1, blocks):
        for h in range(2):
            friends.append((r, h, lax.rem(t + i, blocks)))
    for device in friends:
        pl.semaphore_signal(barrier, inc=1, device_id=device, device_id_type=MESH)
    pl.semaphore_wait(barrier, len(friends))

    def remote(src, dst, send, recv, device):
        return pltpu.make_async_remote_copy(
            src_ref=src, dst_ref=dst, send_sem=send, recv_sem=recv,
            device_id=device, device_id_type=MESH,
        )

    def grad_copy(i):
        sub, c = order[i]
        source = pl.ds(pl.multiple_of(nf * depth + sub * half + c * chunk, chunk), chunk)
        return remote(
            grad_hbm.at[0, :, source, :], peer_grad.at[:, state_rows(sub, c), :],
            grad_send.at[i], grad_recv.at[i], partner,
        )

    def x_own(g, h, sub, slot, device):
        return remote(
            x_hbm.at[some_rows(g), :, features(h, sub)], xbuf.at[t, f, some_rows(g)],
            x_send.at[slot, g], x_recv.at[t, f, g], device,
        )

    def x_swap(g):
        return x_own(g, nf, mine, 0, partner)

    def x_mirror(g, h):
        return x_own(g, h, mine, 1 + h, (r, h, mirror))

    def x_pair(g, h):
        return x_own(g, h, theirs, 3 + h, (r, h, pair))

    def x_pair_mirror(g, h):
        return x_own(g, h, theirs, 5 + h, (r, h, pair_mirror))

    def x_relay(g, th):
        return remote(
            xbuf.at[pair, th, some_rows(g)], xbuf.at[pair, th, some_rows(g)],
            x_send.at[7 + th, g], x_recv.at[pair, th, g], (r, f, mirror),
        )

    def x_arrived(k, th, g):
        remote(
            xbuf.at[k, th, some_rows(g)], xbuf.at[k, th, some_rows(g)],
            x_send.at[0, g], x_recv.at[k, th, g], partner,
        ).wait_recv()

    def x_out(g):
        for h in range(2):
            x_pair(g, h).start()
        for h in range(2):
            x_mirror(g, h).start()

        @pl.when(middle)
        def _():
            for h in range(2):
                x_pair_mirror(g, h).start()

    def relay(g):
        for th in range(2):
            x_arrived(pair, th, g)

        @pl.when(middle)
        def _():
            for th in range(2):
                x_relay(g, th).start()

    def w_pair(c):
        return remote(
            wpair.at[:, pl.ds(c * chunk, chunk), :], wbuf.at[1, :, owner_rows(r, c), :],
            pair_send.at[c], pair_recv.at[c], (r, f, pair),
        )

    def w_copy(cg, c, way):
        return remote(
            wbuf.at[cg, :, owner_rows(r, c), :], wbuf.at[cg, :, owner_rows(r, c), :],
            w_send.at[cg, way, c], w_recv.at[cg, r, c], dev_x if way == 0 else dev_y,
        )

    def w_arrived(cg, owner, c):
        remote(
            wbuf.at[cg, :, owner_rows(owner, c), :], wbuf.at[cg, :, owner_rows(owner, c), :],
            w_send.at[cg, 0, c], w_recv.at[cg, owner, c], dev_x,
        ).wait_recv()

    def w_forward(cg, c):
        owner, device = (rx, dev_y) if c % 2 == 0 else (ry, dev_x)
        return remote(
            wbuf.at[cg, :, owner_rows(owner, c), :], wbuf.at[cg, :, owner_rows(owner, c), :],
            w_fwd_send.at[cg, c], w_recv.at[cg, owner, c], device,
        )

    def w_go(cg, c):
        w_copy(cg, c, 0).start()
        w_copy(cg, c, 1).start()

    def w_step(cg, c):
        w_arrived(cg, rx, c)
        w_arrived(cg, ry, c)
        w_forward(cg, c).start()

    def pair_step(c):
        w_pair(c).wait_recv()
        w_go(1, c)

    grad_copy(0).start()
    x_out(0)
    for i in range(1, len(order)):
        grad_copy(i).start()
    for g in range(GROUPS):
        x_swap(g).start()

    first_bias = 1.0 - 0.9**10
    second_bias = 1.0 - 0.95**10

    def adam(sub, c, out, base):
        def piece(i, carry):
            at = pl.ds(pl.multiple_of(sub * half + c * chunk + i * ADAM_SUB, ADAM_SUB), ADAM_SUB)
            gradient = own_grad[:, at, :].astype(jnp.float32) + peer_grad[:, at, :].astype(jnp.float32)
            new_one = 0.9 * one[:, at, :] + (1.0 - 0.9) * gradient
            new_two = 0.95 * two[:, at, :] + (1.0 - 0.95) * gradient * gradient
            update = new_one / first_bias / (jnp.sqrt(new_two / second_bias) + 1e-08)
            old = master[:, at, :]
            new_master = old - 0.001 * (update + 0.1 * old)
            one[:, at, :] = new_one
            two[:, at, :] = new_two
            master[:, at, :] = new_master
            to = pl.ds(pl.multiple_of(base + c * chunk + i * ADAM_SUB, ADAM_SUB), ADAM_SUB)
            out[:, to, :] = new_master.astype(jnp.bfloat16)
            return carry

        lax.fori_loop(0, chunk // ADAM_SUB, piece, 0)

    for i, (sub, c) in enumerate(order):
        grad_local[i].wait()
        for copy in state_local[i]:
            copy.wait()
        grad_copy(i).wait_recv()
        if i % 2 == 0:
            adam(sub, c, wpair, 0)
            w_pair(c).start()
        else:
            adam(sub, c, wbuf.at[0], r * half)
            if c < W_CHUNKS // 2:
                w_go(0, c)
    for g in range(1, GROUPS):
        x_out(g)
    outs = [
        pltpu.make_async_copy(master, master_out, out_sem.at[0]),
        pltpu.make_async_copy(one, one_out, out_sem.at[1]),
        pltpu.make_async_copy(two, two_out, out_sem.at[2]),
    ]
    for copy in outs:
        copy.start()
    x_local.wait()
    kv_local.wait()

    kv_rows, cache_len = kv_raw.shape[:2]
    pieces = kv_rows // 8

    def split_cache(quarter):
        def body(i, carry):
            row = (quarter * pieces + i) * 2
            at = pl.ds(pl.multiple_of(row * cache_len, 2 * cache_len), 2 * cache_len)
            for j in range(2):
                kv_flat[j, at, :] = kv_raw[pl.ds(row, 2), :, j, :].reshape(2 * cache_len, -1)
            return carry

        lax.fori_loop(0, pieces, body, 0)

    relay(0)
    split_cache(0)
    split_cache(1)
    for c in range(W_CHUNKS // 2):
        w_step(0, c)
    for c in range(W_CHUNKS):
        pair_step(c)
    for c in range(W_CHUNKS // 2, W_CHUNKS):
        w_go(0, c)
    relay(1)
    split_cache(2)
    split_cache(3)
    cached_copy = pltpu.make_async_copy(kv_flat, cached_out, out_sem.at[3])
    cached_copy.start()
    for c in range(W_CHUNKS // 2):
        w_step(1, c)
    relay(2)
    for c in range(W_CHUNKS // 2, W_CHUNKS):
        w_step(1, c)
    relay(3)
    for c in range(W_CHUNKS):
        w_arrived(1, rd, c)

    def far_swap(g):
        return remote(
            far.at[nf, :, tokens(g), :], far_peer.at[:, tokens(g), :], far_send.at[g], far_recv.at[g], partner
        )

    def far_back(g):
        return remote(
            far_out.at[:, tokens(g), :], far_in.at[:, tokens(g), :], back_send.at[g], back_recv.at[g], (r, f, pair)
        )

    def far_step(g, carry):
        x_arrived(t, nf, g)
        for th in range(2):
            x_arrived(mirror, th, g)
            x_arrived(pair_mirror, th, g)

        def flatten(k, inner):
            for th in range(2):
                piece = xbuf[k, th, pl.ds(g * group_rows, group_rows)].reshape(group_tokens, half)
                xflat[th, tokens(g), pl.ds(pl.multiple_of(k * half, half), half)] = piece
            return inner

        lax.fori_loop(0, blocks, flatten, 0)
        lhs = jnp.concatenate([xflat[0, tokens(g), :], xflat[1, tokens(g), :]], axis=0)
        for kv in range(2):
            product = jnp.dot(lhs, wbuf[1, kv], preferred_element_type=jnp.float32)
            for th in range(2):
                far[th, kv, tokens(g), :] = product[th * group_tokens : (th + 1) * group_tokens]
        far_swap(g).start()
        return carry

    def far_done(g):
        far_swap(g).wait_recv()
        far_out[:, tokens(g), :] = far[f, :, tokens(g), :] + far_peer[:, tokens(g), :]
        far_back(g).start()

    def far_loop(g, carry):
        far_step(g, 0)

        @pl.when(g > 0)
        def _():
            far_done(g - 1)

        @pl.when(g == 1)
        def _():
            for c in range(W_CHUNKS // 2, W_CHUNKS):
                w_step(0, c)

        return carry

    lax.fori_loop(0, GROUPS, far_loop, 0)
    far_done(GROUPS - 1)

    def near_step(th, c, first):
        for kv in range(2):
            total = near[th, kv] if not first else None
            for k in range(blocks):
                at = slice(k * half + c * chunk, k * half + (c + 1) * chunk)
                product = jnp.dot(xflat[th, :, at], wbuf[0, kv, at, :], preferred_element_type=jnp.float32)
                total = product if total is None else total + product
            near[th, kv] = total

    near_swap = remote(near.at[nf], near_peer, near_send.at[0], near_recv.at[0], partner)
    for c in range(W_CHUNKS):
        w_arrived(0, rd, c)
        last = c == W_CHUNKS - 1

        def both(i, carry):
            th = jnp.where(i == 0, nf, f)
            near_step(th, c, c == 0)
            if last:
                @pl.when(i == 0)
                def _():
                    near_swap.start()

            return carry

        lax.fori_loop(0, 2, both, 0)

    for i in range(len(order)):
        grad_copy(i).wait_send()
    for c in range(W_CHUNKS):
        w_pair(c).wait_send()
        for cg in range(2):
            w_copy(cg, c, 0).wait_send()
            w_copy(cg, c, 1).wait_send()
            w_forward(cg, c).wait_send()
    for g in range(GROUPS):
        x_swap(g).wait_send()
        for h in range(2):
            x_pair(g, h).wait_send()
            x_mirror(g, h).wait_send()
        far_swap(g).wait_send()
        far_back(g).wait_send()

    @pl.when(middle)
    def _():
        for g in range(GROUPS):
            for h in range(2):
                x_pair_mirror(g, h).wait_send()
                x_relay(g, h).wait_send()

    for copy in outs:
        copy.wait()
    cached_copy.wait()
    for g in range(GROUPS):
        far_back(g).wait_recv()
    near_swap.wait_recv()
    fresh_out[...] = (near[f] + near_peer[...] + far_in[...]).astype(jnp.bfloat16)
    near_swap.wait_send()


def tail_kernel(
    lengths, q_ref, kv_ref, fresh_in, master_in, one_in, two_in,
    context, master_out, one_out, two_out, fresh_ref, sem,
):
    block = pl.program_id(0)
    moves = [
        pltpu.make_async_copy(master_in, master_out, sem.at[1]),
        pltpu.make_async_copy(one_in, one_out, sem.at[2]),
        pltpu.make_async_copy(two_in, two_out, sem.at[3]),
    ]

    @pl.when(block == 0)
    def _():
        fresh_copy = pltpu.make_async_copy(fresh_in, fresh_ref, sem.at[0])
        fresh_copy.start()
        for move in moves:
            move.start()
        fresh_copy.wait()

    step_rows, step_count, features = q_ref.shape
    row_count = TAIL_ROWS
    head = HD
    cache_len = kv_ref.shape[1] // step_rows
    cached = row_count * cache_len
    tokens = row_count * step_count
    keys = cached + tokens
    groups = fresh_ref.shape[2] // head
    per_group = features // head // groups
    column = lax.broadcasted_iota(jnp.int32, (1, keys), 1)
    is_old = column < cached
    new_column = column - cached
    key_row = jnp.where(is_old, column // cache_len, new_column // step_count)
    position = column - key_row * cache_len
    new_row = jnp.where(is_old, -1, key_row)
    token = lax.broadcasted_iota(jnp.int32, (tokens, 1), 0)
    row = token // step_count
    new_valid = (new_row == row) & (new_column <= token)
    low = -0.7 * float(jnp.finfo(jnp.float32).max)
    factor = head**-0.5 * LOG2E
    contract = (((1,), (1,)), ((), ()))
    for part in range(step_rows // row_count):
        first_row = part * row_count
        start = block * step_rows + first_row
        limit = jnp.zeros((1, keys), jnp.int32)
        for at in range(row_count):
            limit = jnp.where(key_row == at, lengths[start + at], limit)
        valid = (jnp.where(is_old & (position < limit), key_row, -1) == row) | new_valid
        here = pl.ds(pl.multiple_of(start * step_count, tokens), tokens)
        old = slice(first_row * cache_len, first_row * cache_len + cached)
        mine = slice(first_row, first_row + row_count)
        for group in range(groups):
            cols = slice(group * head, (group + 1) * head)
            query = jnp.concatenate(
                [
                    q_ref[mine, :, (group * per_group + h) * head : (group * per_group + h + 1) * head].reshape(
                        tokens, head
                    )
                    for h in range(per_group)
                ],
                axis=0,
            )
            key = jnp.concatenate([kv_ref[0, old, cols], fresh_ref[0, here, cols]], axis=0)
            value = jnp.concatenate([kv_ref[1, old, cols], fresh_ref[1, here, cols]], axis=0)
            scores = lax.dot_general(query, key, contract, preferred_element_type=jnp.float32)
            scores = jnp.where(valid[None], scores.reshape(per_group, tokens, keys), low)
            weights = jnp.exp2((scores - jnp.max(scores, axis=-1, keepdims=True)) * factor)
            weights = weights * (1.0 / jnp.sum(weights, axis=-1, keepdims=True))
            weights = weights.astype(jnp.bfloat16).reshape(per_group * tokens, keys)
            out = jnp.dot(weights, value, preferred_element_type=jnp.float32)
            for h in range(per_group):
                at = (group * per_group + h) * head
                piece = out[h * tokens : (h + 1) * tokens].reshape(row_count, step_count, head)
                context[mine, :, at : at + head] = piece.astype(jnp.bfloat16)

    @pl.when(block == pl.num_programs(0) - 1)
    def _():
        for move in moves:
            move.wait()


def fused_device(n_rep, grad_parts, master_weight, moment_one, moment_two, layer_inputs, queries, kv_cache, lengths):
    row_count, step_count, features = layer_inputs.shape
    _, depth, width = master_weight.shape
    n_tp = n_rep
    tokens = row_count * step_count
    cache_len = kv_cache.shape[1]
    bf16, f32 = jnp.bfloat16, jnp.float32
    dma = pltpu.SemaphoreType.DMA
    state = jax.ShapeDtypeStruct(master_weight.shape, f32)
    any_spec = pl.BlockSpec(memory_space=pl.ANY)
    hbm_spec = pl.BlockSpec(memory_space=pltpu.HBM)
    in_place = [
        pltpu.with_memory_space_constraint(array, pltpu.HBM)
        for array in (grad_parts, master_weight, moment_one, moment_two, layer_inputs, kv_cache)
    ]
    half = depth // 2
    fresh, cached, master, one, two = pl.pallas_call(
        learner_kernel,
        out_shape=(
            jax.ShapeDtypeStruct((2, tokens, width), bf16),
            jax.ShapeDtypeStruct((2, row_count * cache_len, width), bf16),
            state,
            state,
            state,
        ),
        in_specs=[hbm_spec] * 6,
        out_specs=(pl.BlockSpec(memory_space=pltpu.VMEM), hbm_spec, any_spec, any_spec, any_spec),
        scratch_shapes=[
            pltpu.VMEM((2, depth, width), bf16),
            pltpu.VMEM((2, depth, width), bf16),
            pltpu.VMEM((2, depth, width), f32),
            pltpu.VMEM((2, depth, width), f32),
            pltpu.VMEM((2, depth, width), f32),
            pltpu.VMEM((2, half, width), bf16),
            pltpu.VMEM((2, 2, n_rep * half, width), bf16),
            pltpu.VMEM((n_tp, 2, row_count, step_count, half), bf16),
            pltpu.VMEM((2, tokens, n_tp * half), bf16),
            pltpu.VMEM((2, 2, tokens, width), f32),
            pltpu.VMEM((2, tokens, width), f32),
            pltpu.VMEM((2, tokens, width), f32),
            pltpu.VMEM((2, tokens, width), f32),
            pltpu.VMEM((2, 2, tokens, width), f32),
            pltpu.VMEM((2, tokens, width), f32),
            pltpu.VMEM(kv_cache.shape, bf16),
            pltpu.VMEM((2, row_count * cache_len, width), bf16),
            dma((2 * W_CHUNKS,)),
            dma((3, 2 * W_CHUNKS)),
            dma((1,)),
            dma((1,)),
            dma((4,)),
            dma((2 * W_CHUNKS,)),
            dma((2 * W_CHUNKS,)),
            dma((9, GROUPS)),
            dma((n_tp, 2, GROUPS)),
            dma((W_CHUNKS,)),
            dma((W_CHUNKS,)),
            dma((2, 2, W_CHUNKS)),
            dma((2, n_rep, W_CHUNKS)),
            dma((2, W_CHUNKS)),
            dma((GROUPS,)),
            dma((GROUPS,)),
            dma((GROUPS,)),
            dma((GROUPS,)),
            dma((1,)),
            dma((1,)),
        ],
        compiler_params=pltpu.CompilerParams(
            collective_id=0, has_side_effects=True, vmem_limit_bytes=36 * 1024 * 1024
        ),
    )(*in_place)
    step_rows = TAIL_ROWS * TAIL_BLOCKS
    token_spec = pl.BlockSpec((step_rows, step_count, features), lambda i, *_: (i, 0, 0))
    context, master, one, two = pl.pallas_call(
        tail_kernel,
        out_shape=(jax.ShapeDtypeStruct(queries.shape, bf16), state, state, state),
        grid_spec=pltpu.PrefetchScalarGridSpec(
            num_scalar_prefetch=1,
            grid=(row_count // step_rows,),
            in_specs=[
                token_spec,
                pl.BlockSpec((2, step_rows * cache_len, width), lambda i, *_: (0, i, 0)),
                any_spec,
                any_spec,
                any_spec,
                any_spec,
            ],
            out_specs=(token_spec, hbm_spec, hbm_spec, hbm_spec),
            scratch_shapes=[pltpu.VMEM((2, tokens, width), bf16), dma((4,))],
        ),
        compiler_params=pltpu.CompilerParams(
            dimension_semantics=("arbitrary",), vmem_limit_bytes=16 * 1024 * 1024
        ),
    )(lengths, queries, cached, fresh, master, one, two)
    return (master, one, two, context)


beta_one = 0.9
beta_two = 0.95
learning_rate = 0.001
weight_decay = 0.1
epsilon = 1e-08
first_bias = 1.0 - 0.9**10
second_bias = 1.0 - 0.95**10


def adamw_update(gradient, master, moment_one, moment_two):
    new_one = beta_one * moment_one + (1.0 - beta_one) * gradient
    new_two = beta_two * moment_two + (1.0 - beta_two) * gradient * gradient
    update = new_one / first_bias / (jnp.sqrt(new_two / second_bias) + epsilon)
    new_master = master - learning_rate * (update + weight_decay * master)
    return (new_one, new_two, new_master)


def attend(queries, kv_cache, fresh_keys, fresh_values, lengths):
    row_count = queries.shape[0]
    step_count = queries.shape[1]
    kv_heads = fresh_keys.shape[2]
    cache_len = kv_cache.shape[1]
    grouped = queries.reshape(row_count, step_count, kv_heads, -1, HD)
    cached_keys = kv_cache[:, :, 0].reshape(row_count, cache_len, kv_heads, HD)
    cached_values = kv_cache[:, :, 1].reshape(row_count, cache_len, kv_heads, HD)
    scaling = 1.0 / jnp.sqrt(jnp.float32(HD))
    cached_scores = (
        jnp.einsum("rsgqd,rcgd->rsgqc", grouped, cached_keys, preferred_element_type=jnp.float32)
        * scaling
    )
    fresh_scores = (
        jnp.einsum("rsgqd,rugd->rsgqu", grouped, fresh_keys, preferred_element_type=jnp.float32)
        * scaling
    )
    valid_old = jnp.arange(cache_len, dtype=jnp.int32)[None, :] < lengths[:, None]
    valid_old = valid_old[:, None, None, None, :]
    steps_index = jnp.arange(step_count, dtype=jnp.int32)
    valid_new = (steps_index[None, :] <= steps_index[:, None])[None, :, None, None, :]
    scores = jnp.concatenate(
        [
            jnp.where(valid_old, cached_scores, -jnp.inf),
            jnp.where(valid_new, fresh_scores, -jnp.inf),
        ],
        axis=-1,
    )
    row_max = jnp.max(scores, axis=-1, keepdims=True)
    exponent = jnp.exp(scores - row_max)
    weights = (exponent / jnp.sum(exponent, axis=-1, keepdims=True)).astype(jnp.bfloat16)
    output = jnp.einsum(
        "rsgqc,rcgd->rsgqd",
        weights[..., :cache_len],
        cached_values,
        preferred_element_type=jnp.float32,
    )
    output = output + jnp.einsum(
        "rsgqu,rugd->rsgqd",
        weights[..., cache_len:],
        fresh_values,
        preferred_element_type=jnp.float32,
    )
    return output.astype(jnp.bfloat16).reshape(row_count, step_count, -1)


def on_device(
    grad_parts, master_weight, moment_one, moment_two, layer_inputs, queries, kv_cache, lengths
):
    gradient = lax.psum_scatter(
        grad_parts[0].astype(jnp.float32).astype(jnp.bfloat16),
        "fsdp",
        scatter_dimension=1,
        tiled=True,
    ).astype(jnp.float32)
    new_one, new_two, new_master = adamw_update(gradient, master_weight, moment_one, moment_two)
    rollout_weight = new_master.astype(jnp.bfloat16)
    row_count = layer_inputs.shape[0]
    step_count = layer_inputs.shape[1]
    gathered = lax.all_gather(layer_inputs, "tp", axis=2, tiled=True)
    flattened = gathered.reshape(row_count * step_count, gathered.shape[2])
    projected = jnp.einsum(
        "td,kdc->ktc",
        flattened,
        lax.all_gather(rollout_weight, ("rep", "fsdp"), axis=1, tiled=True),
        preferred_element_type=jnp.float32,
    )
    fresh_pair = projected.astype(jnp.bfloat16).reshape(2, row_count, step_count, -1, HD)
    context = attend(queries, kv_cache, fresh_pair[0], fresh_pair[1], lengths)
    return (new_master, new_one, new_two, context)


def solution(mesh):
    shape = mesh.shape
    fits = shape["rep"] == 4 and shape["tp"] == 4 and shape["fsdp"] == 2
    run = functools.partial(fused_device, shape["rep"]) if fits else on_device
    return jax.shard_map(
        run,
        mesh=mesh,
        in_specs=(
            P("fsdp", None, "rep", "tp"),
            P(None, ("rep", "fsdp"), "tp"),
            P(None, ("rep", "fsdp"), "tp"),
            P(None, ("rep", "fsdp"), "tp"),
            P(("rep", "fsdp"), None, "tp"),
            P(("rep", "fsdp"), None, "tp"),
            P(("rep", "fsdp"), None, None, "tp"),
            P(("rep", "fsdp")),
        ),
        out_specs=(
            P(None, ("rep", "fsdp"), "tp"),
            P(None, ("rep", "fsdp"), "tp"),
            P(None, ("rep", "fsdp"), "tp"),
            P(("rep", "fsdp"), None, "tp"),
        ),
        check_vma=False,
    )
```

```python
import functools

import jax
import jax.numpy as jnp
from jax import lax
from jax.experimental import pallas as pl
from jax.experimental.pallas import tpu as pltpu
from jax.sharding import PartitionSpec as P

HD = 128
MESH = pl.DeviceIdType.MESH
W_CHUNKS = 4
W_EARLY = 2
GROUPS = 4
ADAM_SUB = 32
TAIL_ROWS = 8
TAIL_BLOCKS = 3
LOG2E = 1.4426950408889634


def learner_kernel(
    grad_hbm, master_hbm, one_hbm, two_hbm, x_hbm, kv_hbm,
    fresh_out, cached_out, master_out, one_out, two_out,
    own_grad, peer_grad, master, one, two, wpair, wbuf, xbuf, xflat,
    far, far_peer, far_out, far_in, near, near_peer, kv_raw, kv_flat,
    grad_sem, state_sem, x_sem, kv_sem, out_sem, grad_send, grad_recv, x_send, x_recv,
    pair_send, pair_recv, w_send, w_recv, w_fwd_send, far_send, far_recv, back_send, back_recv, near_send, near_recv,
):
    r, f, t = lax.axis_index("rep"), lax.axis_index("fsdp"), lax.axis_index("tp")
    nf = 1 - f
    rx = r + 1 - 2 * lax.rem(r, 2)
    ry = lax.rem(r + 2, 4)
    rd = lax.rem(rx + 2, 4)
    partner, dev_x, dev_y = (r, nf, t), (rx, f, t), (ry, f, t)
    pair = t + 1 - 2 * lax.rem(t, 2)
    mirror = 3 - t
    pair_mirror = 3 - pair
    middle = (t == 1) | (t == 2)
    mine = lax.rem((t + 1) // 2, 2)
    theirs = 1 - mine
    depth = master.shape[1]
    half = depth // 2
    chunk = half // W_CHUNKS
    x_rows, x_steps = xbuf.shape[2:4]
    group_rows = x_rows // GROUPS
    group_tokens = group_rows * x_steps
    blocks = wbuf.shape[2] // half

    def state_rows(sub, c):
        return pl.ds(pl.multiple_of(sub * half + c * chunk, chunk), chunk)

    def owner_rows(owner, c):
        return pl.ds(pl.multiple_of(owner * half + c * chunk, chunk), chunk)

    order = []
    for c in range(W_CHUNKS):
        order += [(theirs, c), (mine, c)]

    def features(h, sub):
        return pl.ds(pl.multiple_of(h * depth + sub * half, half), half)

    def some_rows(g):
        return pl.ds(g * group_rows, group_rows)

    def tokens(g):
        return pl.ds(pl.multiple_of(g * group_tokens, group_tokens), group_tokens)

    grad_local, state_local = [], []
    for i, (sub, c) in enumerate(order):
        at = state_rows(sub, c)
        source = pl.ds(pl.multiple_of(f * depth + sub * half + c * chunk, chunk), chunk)
        grad_local.append(
            pltpu.make_async_copy(grad_hbm.at[0, :, source, :], own_grad.at[:, at, :], grad_sem.at[i])
        )
        state_local.append([
            pltpu.make_async_copy(hbm.at[:, at, :], vmem.at[:, at, :], state_sem.at[j, i])
            for j, (hbm, vmem) in enumerate(((master_hbm, master), (one_hbm, one), (two_hbm, two)))
        ])
        grad_local[i].start()
        for copy in state_local[i]:
            copy.start()
    x_local = pltpu.make_async_copy(x_hbm.at[:, :, features(f, mine)], xbuf.at[t, f], x_sem.at[0])
    kv_local = pltpu.make_async_copy(kv_hbm, kv_raw, kv_sem.at[0])
    x_local.start()
    kv_local.start()

    barrier = pltpu.get_barrier_semaphore()
    friends = [partner, dev_x, dev_y]
    for i in range(1, blocks):
        for h in range(2):
            friends.append((r, h, lax.rem(t + i, blocks)))
    for device in friends:
        pl.semaphore_signal(barrier, inc=1, device_id=device, device_id_type=MESH)
    pl.semaphore_wait(barrier, len(friends))

    def remote(src, dst, send, recv, device):
        return pltpu.make_async_remote_copy(
            src_ref=src, dst_ref=dst, send_sem=send, recv_sem=recv,
            device_id=device, device_id_type=MESH,
        )

    def grad_copy(i):
        sub, c = order[i]
        source = pl.ds(pl.multiple_of(nf * depth + sub * half + c * chunk, chunk), chunk)
        return remote(
            grad_hbm.at[0, :, source, :], peer_grad.at[:, state_rows(sub, c), :],
            grad_send.at[i], grad_recv.at[i], partner,
        )

    def x_own(g, h, sub, slot, device):
        return remote(
            x_hbm.at[some_rows(g), :, features(h, sub)], xbuf.at[t, f, some_rows(g)],
            x_send.at[slot, g], x_recv.at[t, f, g], device,
        )

    def x_swap(g):
        return x_own(g, nf, mine, 0, partner)

    def x_mirror(g, h):
        return x_own(g, h, mine, 1 + h, (r, h, mirror))

    def x_pair(g, h):
        return x_own(g, h, theirs, 3 + h, (r, h, pair))

    def x_pair_mirror(g, h):
        return x_own(g, h, theirs, 5 + h, (r, h, pair_mirror))

    def x_relay(g, th):
        return remote(
            xbuf.at[pair, th, some_rows(g)], xbuf.at[pair, th, some_rows(g)],
            x_send.at[7 + th, g], x_recv.at[pair, th, g], (r, f, mirror),
        )

    def x_arrived(k, th, g):
        remote(
            xbuf.at[k, th, some_rows(g)], xbuf.at[k, th, some_rows(g)],
            x_send.at[0, g], x_recv.at[k, th, g], partner,
        ).wait_recv()

    def go(make, groups):
        for g in groups:
            for h in range(2):
                make(g, h).start()

    every = range(GROUPS)
    early = range(GROUPS // 2)
    late = range(GROUPS // 2, GROUPS)

    def relay(g):
        for th in range(2):
            x_arrived(pair, th, g)

        for th in range(2):
            x_relay(g, th).start()

    def w_pair(c):
        return remote(
            wpair.at[:, pl.ds(c * chunk, chunk), :], wbuf.at[1, :, owner_rows(r, c), :],
            pair_send.at[c], pair_recv.at[c], (r, f, pair),
        )

    def w_copy(cg, c, way):
        return remote(
            wbuf.at[cg, :, owner_rows(r, c), :], wbuf.at[cg, :, owner_rows(r, c), :],
            w_send.at[cg, way, c], w_recv.at[cg, r, c], dev_x if way == 0 else dev_y,
        )

    def w_arrived(cg, owner, c):
        remote(
            wbuf.at[cg, :, owner_rows(owner, c), :], wbuf.at[cg, :, owner_rows(owner, c), :],
            w_send.at[cg, 0, c], w_recv.at[cg, owner, c], dev_x,
        ).wait_recv()

    def w_forward(cg, c):
        owner, device = (rx, dev_y) if c % 2 == 0 else (ry, dev_x)
        return remote(
            wbuf.at[cg, :, owner_rows(owner, c), :], wbuf.at[cg, :, owner_rows(owner, c), :],
            w_fwd_send.at[cg, c], w_recv.at[cg, owner, c], device,
        )

    def w_go(cg, c):
        w_copy(cg, c, 0).start()
        w_copy(cg, c, 1).start()

    def w_step(cg, c):
        w_arrived(cg, rx, c)
        w_arrived(cg, ry, c)
        w_forward(cg, c).start()

    def pair_step(c):
        w_pair(c).wait_recv()
        w_go(1, c)

    grad_copy(0).start()

    @pl.when(middle)
    def _():
        go(x_mirror, every)
        go(x_pair, early)

    @pl.when(jnp.logical_not(middle))
    def _():
        go(x_pair, early)

    for i in range(1, len(order)):
        grad_copy(i).start()
    for g in range(GROUPS):
        x_swap(g).start()

    first_bias = 1.0 - 0.9**10
    second_bias = 1.0 - 0.95**10

    def adam(sub, c, out, base):
        def piece(i, carry):
            at = pl.ds(pl.multiple_of(sub * half + c * chunk + i * ADAM_SUB, ADAM_SUB), ADAM_SUB)
            gradient = own_grad[:, at, :].astype(jnp.float32) + peer_grad[:, at, :].astype(jnp.float32)
            new_one = 0.9 * one[:, at, :] + (1.0 - 0.9) * gradient
            new_two = 0.95 * two[:, at, :] + (1.0 - 0.95) * gradient * gradient
            update = new_one / first_bias / (jnp.sqrt(new_two / second_bias) + 1e-08)
            old = master[:, at, :]
            new_master = old - 0.001 * (update + 0.1 * old)
            one[:, at, :] = new_one
            two[:, at, :] = new_two
            master[:, at, :] = new_master
            to = pl.ds(pl.multiple_of(base + c * chunk + i * ADAM_SUB, ADAM_SUB), ADAM_SUB)
            out[:, to, :] = new_master.astype(jnp.bfloat16)
            return carry

        lax.fori_loop(0, chunk // ADAM_SUB, piece, 0)

    for i, (sub, c) in enumerate(order):
        grad_local[i].wait()
        for copy in state_local[i]:
            copy.wait()
        grad_copy(i).wait_recv()
        if i % 2 == 0:
            adam(sub, c, wpair, 0)
            w_pair(c).start()
        else:
            adam(sub, c, wbuf.at[0], r * half)
            if c < W_EARLY:
                w_go(0, c)

    outs = [
        pltpu.make_async_copy(master, master_out, out_sem.at[0]),
        pltpu.make_async_copy(one, one_out, out_sem.at[1]),
        pltpu.make_async_copy(two, two_out, out_sem.at[2]),
    ]
    for copy in outs:
        copy.start()
    x_local.wait()
    kv_local.wait()

    kv_rows, cache_len = kv_raw.shape[:2]
    pieces = kv_rows // 8

    def split_cache(quarter):
        def body(i, carry):
            row = (quarter * pieces + i) * 2
            at = pl.ds(pl.multiple_of(row * cache_len, 2 * cache_len), 2 * cache_len)
            for j in range(2):
                kv_flat[j, at, :] = kv_raw[pl.ds(row, 2), :, j, :].reshape(2 * cache_len, -1)
            return carry

        lax.fori_loop(0, pieces, body, 0)

    @pl.when(middle)
    def _():
        for g in early:
            relay(g)

    @pl.when(jnp.logical_not(middle))
    def _():
        go(x_pair, late)

    def send_next(item):
        cg, c = item
        if cg == 1:
            pair_step(c)
        else:
            w_go(0, c)

    items = [(0, c) for c in range(W_EARLY)] + [(1, c) for c in range(W_CHUNKS)]
    items += [(0, c) for c in range(W_EARLY, W_CHUNKS)]
    for i in range(W_EARLY + W_CHUNKS):
        w_step(*items[i])
        if i + W_EARLY < len(items):
            send_next(items[i + W_EARLY])
            if items[i + W_EARLY] == (1, W_CHUNKS - 1):
                @pl.when(middle)
                def _():
                    go(x_pair, late)
                    go(x_pair_mirror, early)

                @pl.when(jnp.logical_not(middle))
                def _():
                    go(x_mirror, every)

        if i < 4:
            split_cache(i)
        if i == W_CHUNKS:
            @pl.when(middle)
            def _():
                for g in late:
                    relay(g)
                go(x_pair_mirror, late)
    cached_copy = pltpu.make_async_copy(kv_flat, cached_out, out_sem.at[3])
    cached_copy.start()
    for c in range(W_CHUNKS):
        w_arrived(1, rd, c)
    for c in range(W_EARLY):
        w_arrived(0, rd, c)
    for c in range(W_EARLY, W_CHUNKS - 1):
        w_step(0, c)

    def far_swap(g):
        return remote(
            far.at[nf, :, tokens(g), :], far_peer.at[:, tokens(g), :], far_send.at[g], far_recv.at[g], partner
        )

    def far_back(g):
        return remote(
            far_out.at[:, tokens(g), :], far_in.at[:, tokens(g), :], back_send.at[g], back_recv.at[g], (r, f, pair)
        )

    def near_part(lhs, kv, start, stop):
        total = None
        for k in range(blocks):
            at = slice(k * half + start * chunk, k * half + stop * chunk)
            product = jnp.dot(lhs[:, at], wbuf[0, kv, at, :], preferred_element_type=jnp.float32)
            total = product if total is None else total + product
        return total

    def far_step(g, carry):
        @pl.when(jnp.logical_not(middle))
        def _():
            for th in range(2):
                x_arrived(pair, th, g)

        x_arrived(t, nf, g)
        for th in range(2):
            x_arrived(mirror, th, g)
            x_arrived(pair_mirror, th, g)

        def flatten(k, inner):
            for th in range(2):
                piece = xbuf[k, th, pl.ds(g * group_rows, group_rows)].reshape(group_tokens, half)
                xflat[th, tokens(g), pl.ds(pl.multiple_of(k * half, half), half)] = piece
            return inner

        lax.fori_loop(0, blocks, flatten, 0)
        lhs = jnp.concatenate([xflat[0, tokens(g), :], xflat[1, tokens(g), :]], axis=0)
        for kv in range(2):
            product = jnp.dot(lhs, wbuf[1, kv], preferred_element_type=jnp.float32)
            for th in range(2):
                far[th, kv, tokens(g), :] = product[th * group_tokens : (th + 1) * group_tokens]
        far_swap(g).start()
        for kv in range(2):
            product = near_part(lhs, kv, 0, W_EARLY)
            for th in range(2):
                near[th, kv, tokens(g), :] = product[th * group_tokens : (th + 1) * group_tokens]
        return carry

    def far_done(g):
        far_swap(g).wait_recv()
        both = far[f, :, tokens(g), :] + far_peer[:, tokens(g), :]
        far_out[:, tokens(g), :] = both.astype(jnp.bfloat16)
        far_back(g).start()

    def far_loop(g, carry):
        far_step(g, 0)

        @pl.when(g > 0)
        def _():
            far_done(g - 1)

        @pl.when(g == 0)
        def _():
            w_step(0, W_CHUNKS - 1)

        return carry

    lax.fori_loop(0, GROUPS, far_loop, 0)
    far_done(GROUPS - 1)

    near_swap = remote(near.at[nf], near_peer, near_send.at[0], near_recv.at[0], partner)
    for c in range(W_EARLY, W_CHUNKS):
        w_arrived(0, rd, c)

    def near_last(i, carry):
        th = jnp.where(i == 0, nf, f)
        for kv in range(2):
            near[th, kv] += near_part(xflat.at[th], kv, W_EARLY, W_CHUNKS)

        @pl.when(i == 0)
        def _():
            near_swap.start()

        return carry

    lax.fori_loop(0, 2, near_last, 0)

    for i in range(len(order)):
        grad_copy(i).wait_send()
    for c in range(W_CHUNKS):
        w_pair(c).wait_send()
        for cg in range(2):
            w_copy(cg, c, 0).wait_send()
            w_copy(cg, c, 1).wait_send()
            w_forward(cg, c).wait_send()
    for g in range(GROUPS):
        x_swap(g).wait_send()
        for h in range(2):
            x_pair(g, h).wait_send()
            x_mirror(g, h).wait_send()
        far_swap(g).wait_send()
        far_back(g).wait_send()

    @pl.when(middle)
    def _():
        for g in range(GROUPS):
            for h in range(2):
                x_pair_mirror(g, h).wait_send()
                x_relay(g, h).wait_send()

    for copy in outs:
        copy.wait()
    cached_copy.wait()
    for g in range(GROUPS):
        far_back(g).wait_recv()
    near_swap.wait_recv()
    fresh_out[...] = (near[f] + near_peer[...] + far_in[...].astype(jnp.float32)).astype(jnp.bfloat16)
    near_swap.wait_send()


def tail_kernel(
    lengths, q_ref, kv_ref, fresh_in, master_in, one_in, two_in,
    context, master_out, one_out, two_out, fresh_ref, sem,
):
    block = pl.program_id(0)
    moves = [
        pltpu.make_async_copy(master_in, master_out, sem.at[1]),
        pltpu.make_async_copy(one_in, one_out, sem.at[2]),
        pltpu.make_async_copy(two_in, two_out, sem.at[3]),
    ]

    @pl.when(block == 0)
    def _():
        fresh_copy = pltpu.make_async_copy(fresh_in, fresh_ref, sem.at[0])
        fresh_copy.start()
        for move in moves:
            move.start()
        fresh_copy.wait()

    step_rows, step_count, features = q_ref.shape
    row_count = TAIL_ROWS
    head = HD
    cache_len = kv_ref.shape[1] // step_rows
    cached = row_count * cache_len
    tokens = row_count * step_count
    keys = cached + tokens
    groups = fresh_ref.shape[2] // head
    per_group = features // head // groups
    column = lax.broadcasted_iota(jnp.int32, (1, keys), 1)
    is_old = column < cached
    new_column = column - cached
    key_row = jnp.where(is_old, column // cache_len, new_column // step_count)
    position = column - key_row * cache_len
    new_row = jnp.where(is_old, -1, key_row)
    token = lax.broadcasted_iota(jnp.int32, (tokens, 1), 0)
    row = token // step_count
    new_valid = (new_row == row) & (new_column <= token)
    low = -0.7 * float(jnp.finfo(jnp.float32).max)
    factor = head**-0.5 * LOG2E
    contract = (((1,), (1,)), ((), ()))
    for part in range(step_rows // row_count):
        first_row = part * row_count
        start = block * step_rows + first_row
        limit = jnp.zeros((1, keys), jnp.int32)
        for at in range(row_count):
            limit = jnp.where(key_row == at, lengths[start + at], limit)
        valid = (jnp.where(is_old & (position < limit), key_row, -1) == row) | new_valid
        here = pl.ds(pl.multiple_of(start * step_count, tokens), tokens)
        old = slice(first_row * cache_len, first_row * cache_len + cached)
        mine = slice(first_row, first_row + row_count)
        for group in range(groups):
            cols = slice(group * head, (group + 1) * head)
            query = jnp.concatenate(
                [
                    q_ref[mine, :, (group * per_group + h) * head : (group * per_group + h + 1) * head].reshape(
                        tokens, head
                    )
                    for h in range(per_group)
                ],
                axis=0,
            )
            key = jnp.concatenate([kv_ref[0, old, cols], fresh_ref[0, here, cols]], axis=0)
            value = jnp.concatenate([kv_ref[1, old, cols], fresh_ref[1, here, cols]], axis=0)
            scores = lax.dot_general(query, key, contract, preferred_element_type=jnp.float32)
            scores = jnp.where(valid[None], scores.reshape(per_group, tokens, keys), low)
            weights = jnp.exp2((scores - jnp.max(scores, axis=-1, keepdims=True)) * factor)
            weights = weights * (1.0 / jnp.sum(weights, axis=-1, keepdims=True))
            weights = weights.astype(jnp.bfloat16).reshape(per_group * tokens, keys)
            out = jnp.dot(weights, value, preferred_element_type=jnp.float32)
            for h in range(per_group):
                at = (group * per_group + h) * head
                piece = out[h * tokens : (h + 1) * tokens].reshape(row_count, step_count, head)
                context[mine, :, at : at + head] = piece.astype(jnp.bfloat16)

    @pl.when(block == pl.num_programs(0) - 1)
    def _():
        for move in moves:
            move.wait()


def fused_device(n_rep, grad_parts, master_weight, moment_one, moment_two, layer_inputs, queries, kv_cache, lengths):
    row_count, step_count, features = layer_inputs.shape
    _, depth, width = master_weight.shape
    n_tp = n_rep
    tokens = row_count * step_count
    cache_len = kv_cache.shape[1]
    bf16, f32 = jnp.bfloat16, jnp.float32
    dma = pltpu.SemaphoreType.DMA
    state = jax.ShapeDtypeStruct(master_weight.shape, f32)
    any_spec = pl.BlockSpec(memory_space=pl.ANY)
    hbm_spec = pl.BlockSpec(memory_space=pltpu.HBM)
    in_place = [
        pltpu.with_memory_space_constraint(array, pltpu.HBM)
        for array in (grad_parts, master_weight, moment_one, moment_two, layer_inputs, kv_cache)
    ]
    half = depth // 2
    fresh, cached, master, one, two = pl.pallas_call(
        learner_kernel,
        out_shape=(
            jax.ShapeDtypeStruct((2, tokens, width), bf16),
            jax.ShapeDtypeStruct((2, row_count * cache_len, width), bf16),
            state,
            state,
            state,
        ),
        in_specs=[hbm_spec] * 6,
        out_specs=(pl.BlockSpec(memory_space=pltpu.VMEM), hbm_spec, any_spec, any_spec, any_spec),
        scratch_shapes=[
            pltpu.VMEM((2, depth, width), bf16),
            pltpu.VMEM((2, depth, width), bf16),
            pltpu.VMEM((2, depth, width), f32),
            pltpu.VMEM((2, depth, width), f32),
            pltpu.VMEM((2, depth, width), f32),
            pltpu.VMEM((2, half, width), bf16),
            pltpu.VMEM((2, 2, n_rep * half, width), bf16),
            pltpu.VMEM((n_tp, 2, row_count, step_count, half), bf16),
            pltpu.VMEM((2, tokens, n_tp * half), bf16),
            pltpu.VMEM((2, 2, tokens, width), f32),
            pltpu.VMEM((2, tokens, width), f32),
            pltpu.VMEM((2, tokens, width), bf16),
            pltpu.VMEM((2, tokens, width), bf16),
            pltpu.VMEM((2, 2, tokens, width), f32),
            pltpu.VMEM((2, tokens, width), f32),
            pltpu.VMEM(kv_cache.shape, bf16),
            pltpu.VMEM((2, row_count * cache_len, width), bf16),
            dma((2 * W_CHUNKS,)),
            dma((3, 2 * W_CHUNKS)),
            dma((1,)),
            dma((1,)),
            dma((4,)),
            dma((2 * W_CHUNKS,)),
            dma((2 * W_CHUNKS,)),
            dma((9, GROUPS)),
            dma((n_tp, 2, GROUPS)),
            dma((W_CHUNKS,)),
            dma((W_CHUNKS,)),
            dma((2, 2, W_CHUNKS)),
            dma((2, n_rep, W_CHUNKS)),
            dma((2, W_CHUNKS)),
            dma((GROUPS,)),
            dma((GROUPS,)),
            dma((GROUPS,)),
            dma((GROUPS,)),
            dma((1,)),
            dma((1,)),
        ],
        compiler_params=pltpu.CompilerParams(
            collective_id=0, has_side_effects=True, vmem_limit_bytes=36 * 1024 * 1024
        ),
    )(*in_place)
    step_rows = TAIL_ROWS * TAIL_BLOCKS
    token_spec = pl.BlockSpec((step_rows, step_count, features), lambda i, *_: (i, 0, 0))
    context, master, one, two = pl.pallas_call(
        tail_kernel,
        out_shape=(jax.ShapeDtypeStruct(queries.shape, bf16), state, state, state),
        grid_spec=pltpu.PrefetchScalarGridSpec(
            num_scalar_prefetch=1,
            grid=(row_count // step_rows,),
            in_specs=[
                token_spec,
                pl.BlockSpec((2, step_rows * cache_len, width), lambda i, *_: (0, i, 0)),
                any_spec,
                any_spec,
                any_spec,
                any_spec,
            ],
            out_specs=(token_spec, hbm_spec, hbm_spec, hbm_spec),
            scratch_shapes=[pltpu.VMEM((2, tokens, width), bf16), dma((4,))],
        ),
        compiler_params=pltpu.CompilerParams(
            dimension_semantics=("arbitrary",), vmem_limit_bytes=16 * 1024 * 1024
        ),
    )(lengths, queries, cached, fresh, master, one, two)
    return (master, one, two, context)


beta_one = 0.9
beta_two = 0.95
learning_rate = 0.001
weight_decay = 0.1
epsilon = 1e-08
first_bias = 1.0 - 0.9**10
second_bias = 1.0 - 0.95**10


def adamw_update(gradient, master, moment_one, moment_two):
    new_one = beta_one * moment_one + (1.0 - beta_one) * gradient
    new_two = beta_two * moment_two + (1.0 - beta_two) * gradient * gradient
    update = new_one / first_bias / (jnp.sqrt(new_two / second_bias) + epsilon)
    new_master = master - learning_rate * (update + weight_decay * master)
    return (new_one, new_two, new_master)


def attend(queries, kv_cache, fresh_keys, fresh_values, lengths):
    row_count = queries.shape[0]
    step_count = queries.shape[1]
    kv_heads = fresh_keys.shape[2]
    cache_len = kv_cache.shape[1]
    grouped = queries.reshape(row_count, step_count, kv_heads, -1, HD)
    cached_keys = kv_cache[:, :, 0].reshape(row_count, cache_len, kv_heads, HD)
    cached_values = kv_cache[:, :, 1].reshape(row_count, cache_len, kv_heads, HD)
    scaling = 1.0 / jnp.sqrt(jnp.float32(HD))
    cached_scores = (
        jnp.einsum("rsgqd,rcgd->rsgqc", grouped, cached_keys, preferred_element_type=jnp.float32)
        * scaling
    )
    fresh_scores = (
        jnp.einsum("rsgqd,rugd->rsgqu", grouped, fresh_keys, preferred_element_type=jnp.float32)
        * scaling
    )
    valid_old = jnp.arange(cache_len, dtype=jnp.int32)[None, :] < lengths[:, None]
    valid_old = valid_old[:, None, None, None, :]
    steps_index = jnp.arange(step_count, dtype=jnp.int32)
    valid_new = (steps_index[None, :] <= steps_index[:, None])[None, :, None, None, :]
    scores = jnp.concatenate(
        [
            jnp.where(valid_old, cached_scores, -jnp.inf),
            jnp.where(valid_new, fresh_scores, -jnp.inf),
        ],
        axis=-1,
    )
    row_max = jnp.max(scores, axis=-1, keepdims=True)
    exponent = jnp.exp(scores - row_max)
    weights = (exponent / jnp.sum(exponent, axis=-1, keepdims=True)).astype(jnp.bfloat16)
    output = jnp.einsum(
        "rsgqc,rcgd->rsgqd",
        weights[..., :cache_len],
        cached_values,
        preferred_element_type=jnp.float32,
    )
    output = output + jnp.einsum(
        "rsgqu,rugd->rsgqd",
        weights[..., cache_len:],
        fresh_values,
        preferred_element_type=jnp.float32,
    )
    return output.astype(jnp.bfloat16).reshape(row_count, step_count, -1)


def on_device(
    grad_parts, master_weight, moment_one, moment_two, layer_inputs, queries, kv_cache, lengths
):
    gradient = lax.psum_scatter(
        grad_parts[0].astype(jnp.float32).astype(jnp.bfloat16),
        "fsdp",
        scatter_dimension=1,
        tiled=True,
    ).astype(jnp.float32)
    new_one, new_two, new_master = adamw_update(gradient, master_weight, moment_one, moment_two)
    rollout_weight = new_master.astype(jnp.bfloat16)
    row_count = layer_inputs.shape[0]
    step_count = layer_inputs.shape[1]
    gathered = lax.all_gather(layer_inputs, "tp", axis=2, tiled=True)
    flattened = gathered.reshape(row_count * step_count, gathered.shape[2])
    projected = jnp.einsum(
        "td,kdc->ktc",
        flattened,
        lax.all_gather(rollout_weight, ("rep", "fsdp"), axis=1, tiled=True),
        preferred_element_type=jnp.float32,
    )
    fresh_pair = projected.astype(jnp.bfloat16).reshape(2, row_count, step_count, -1, HD)
    context = attend(queries, kv_cache, fresh_pair[0], fresh_pair[1], lengths)
    return (new_master, new_one, new_two, context)


def solution(mesh):
    shape = mesh.shape
    fits = shape["rep"] == 4 and shape["tp"] == 4 and shape["fsdp"] == 2
    run = functools.partial(fused_device, shape["rep"]) if fits else on_device
    return jax.shard_map(
        run,
        mesh=mesh,
        in_specs=(
            P("fsdp", None, "rep", "tp"),
            P(None, ("rep", "fsdp"), "tp"),
            P(None, ("rep", "fsdp"), "tp"),
            P(None, ("rep", "fsdp"), "tp"),
            P(("rep", "fsdp"), None, "tp"),
            P(("rep", "fsdp"), None, "tp"),
            P(("rep", "fsdp"), None, None, "tp"),
            P(("rep", "fsdp")),
        ),
        out_specs=(
            P(None, ("rep", "fsdp"), "tp"),
            P(None, ("rep", "fsdp"), "tp"),
            P(None, ("rep", "fsdp"), "tp"),
            P(("rep", "fsdp"), None, "tp"),
        ),
        check_vma=False,
    )
```

```python
import functools

import jax
import jax.numpy as jnp
from jax import lax
from jax.experimental import pallas as pl
from jax.experimental.pallas import tpu as pltpu
from jax.sharding import PartitionSpec as P

HD = 128
MESH = pl.DeviceIdType.MESH
W_CHUNKS = 4
W_EARLY = 2
GROUPS = 4
ADAM_SUB = 32
TAIL_ROWS = 8
LOG2E = 1.4426950408889634
LOW = -0.7 * 3.4028234663852886e38


def learner_kernel(
    lengths_hbm, grad_hbm, master_hbm, one_hbm, two_hbm, x_hbm, kv_hbm, q_hbm,
    fresh_out, query_out, old_out, mass_out, master_out, one_out, two_out,
    own_grad, peer_grad, master, one, two, wpair, wbuf, xbuf, xflat,
    far, far_peer, far_out, far_in, near, near_peer, kv_raw, q_raw, lengths, xstage,
    grad_sem, state_sem, x_sem, kv_sem, out_sem, grad_send, grad_recv, x_send, x_recv, stage_send, stage_recv,
    pair_send, pair_recv, w_send, w_recv, w_fwd_send, far_send, far_recv, back_send, back_recv, near_send, near_recv,
):
    r, f, t = lax.axis_index("rep"), lax.axis_index("fsdp"), lax.axis_index("tp")
    nf = 1 - f
    rx = r + 1 - 2 * lax.rem(r, 2)
    ry = lax.rem(r + 2, 4)
    rd = lax.rem(rx + 2, 4)
    partner, dev_x, dev_y = (r, nf, t), (rx, f, t), (ry, f, t)
    pair = t + 1 - 2 * lax.rem(t, 2)
    mirror = 3 - t
    pair_mirror = 3 - pair
    middle = (t == 1) | (t == 2)
    mine = lax.rem((t + 1) // 2, 2)
    theirs = 1 - mine
    depth = master.shape[1]
    half = depth // 2
    chunk = half // W_CHUNKS
    x_rows, x_steps = xbuf.shape[2:4]
    group_rows = x_rows // GROUPS
    group_tokens = group_rows * x_steps
    blocks = wbuf.shape[2] // half

    def state_rows(sub, c):
        return pl.ds(pl.multiple_of(sub * half + c * chunk, chunk), chunk)

    def owner_rows(owner, c):
        return pl.ds(pl.multiple_of(owner * half + c * chunk, chunk), chunk)

    order = []
    for c in range(W_CHUNKS):
        order += [(theirs, c), (mine, c)]

    def features(h, sub):
        return pl.ds(pl.multiple_of(h * depth + sub * half, half), half)

    def some_rows(g):
        return pl.ds(g * group_rows, group_rows)

    def tokens(g):
        return pl.ds(pl.multiple_of(g * group_tokens, group_tokens), group_tokens)

    grad_local, state_local = [], []
    for i, (sub, c) in enumerate(order):
        at = state_rows(sub, c)
        source = pl.ds(pl.multiple_of(f * depth + sub * half + c * chunk, chunk), chunk)
        grad_local.append(
            pltpu.make_async_copy(grad_hbm.at[0, :, source, :], own_grad.at[:, at, :], grad_sem.at[i])
        )
        state_local.append([
            pltpu.make_async_copy(hbm.at[:, at, :], vmem.at[:, at, :], state_sem.at[j, i])
            for j, (hbm, vmem) in enumerate(((master_hbm, master), (one_hbm, one), (two_hbm, two)))
        ])
        grad_local[i].start()
        for copy in state_local[i]:
            copy.start()
    x_local = pltpu.make_async_copy(x_hbm.at[:, :, features(f, mine)], xbuf.at[t, f], x_sem.at[0])
    kv_local = pltpu.make_async_copy(kv_hbm, kv_raw, kv_sem.at[0])
    x_local.start()
    kv_local.start()
    q_local = pltpu.make_async_copy(q_hbm, q_raw, kv_sem.at[1])
    q_local.start()
    length_local = pltpu.make_async_copy(lengths_hbm, lengths, kv_sem.at[2])
    length_local.start()

    barrier = pltpu.get_barrier_semaphore()
    friends = [partner, dev_x, dev_y]
    for i in range(1, blocks):
        for h in range(2):
            friends.append((r, h, lax.rem(t + i, blocks)))
    for device in friends:
        pl.semaphore_signal(barrier, inc=1, device_id=device, device_id_type=MESH)
    pl.semaphore_wait(barrier, len(friends))

    def remote(src, dst, send, recv, device):
        return pltpu.make_async_remote_copy(
            src_ref=src, dst_ref=dst, send_sem=send, recv_sem=recv,
            device_id=device, device_id_type=MESH,
        )

    def grad_copy(i):
        sub, c = order[i]
        source = pl.ds(pl.multiple_of(nf * depth + sub * half + c * chunk, chunk), chunk)
        return remote(
            grad_hbm.at[0, :, source, :], peer_grad.at[:, state_rows(sub, c), :],
            grad_send.at[i], grad_recv.at[i], partner,
        )

    def x_own(g, h, sub, slot, device):
        return remote(
            x_hbm.at[some_rows(g), :, features(h, sub)], xbuf.at[t, f, some_rows(g)],
            x_send.at[slot, g], x_recv.at[t, f, g], device,
        )

    def x_swap(g):
        return x_own(g, nf, mine, 0, partner)

    def x_mirror(g, h):
        return x_own(g, h, mine, 1 + h, (r, h, mirror))

    def x_pair(g, h):
        return x_own(g, h, theirs, 3 + h, (r, h, pair))

    def x_pair_mirror(g, h):
        return x_own(g, h, theirs, 5 + h, (r, h, pair_mirror))

    def x_relay(g, th):
        return remote(
            xbuf.at[pair, th, some_rows(g)], xbuf.at[pair, th, some_rows(g)],
            x_send.at[7 + th, g], x_recv.at[pair, th, g], (r, f, mirror),
        )

    def x_stage(g, h):
        return remote(
            x_hbm.at[some_rows(g), :, features(h, theirs)], xstage.at[f, some_rows(g)],
            x_send.at[5 + h, g], stage_recv.at[f, g], (r, h, mirror),
        )

    def x_unstage(g, th):
        return remote(
            xstage.at[th, some_rows(g)], xbuf.at[mirror, th, some_rows(g)],
            stage_send.at[th, g], x_recv.at[mirror, th, g], (r, f, pair),
        )

    def unstage(g):
        for th in range(2):
            remote(
                xstage.at[th, some_rows(g)], xstage.at[th, some_rows(g)],
                x_send.at[5, g], stage_recv.at[th, g], (r, f, mirror),
            ).wait_recv()
            x_unstage(g, th).start()

    def x_arrived(k, th, g):
        remote(
            xbuf.at[k, th, some_rows(g)], xbuf.at[k, th, some_rows(g)],
            x_send.at[0, g], x_recv.at[k, th, g], partner,
        ).wait_recv()

    def go(make, groups):
        for g in groups:
            for h in range(2):
                make(g, h).start()

    every = range(GROUPS)
    early = range(GROUPS // 2)
    late = range(GROUPS // 2, GROUPS)

    def relay(g):
        for th in range(2):
            x_arrived(pair, th, g)

        for th in range(2):
            x_relay(g, th).start()

    def w_pair(c):
        return remote(
            wpair.at[:, pl.ds(c * chunk, chunk), :], wbuf.at[1, :, owner_rows(r, c), :],
            pair_send.at[c], pair_recv.at[c], (r, f, pair),
        )

    def w_copy(cg, c, way):
        return remote(
            wbuf.at[cg, :, owner_rows(r, c), :], wbuf.at[cg, :, owner_rows(r, c), :],
            w_send.at[cg, way, c], w_recv.at[cg, r, c], dev_x if way == 0 else dev_y,
        )

    def w_arrived(cg, owner, c):
        remote(
            wbuf.at[cg, :, owner_rows(owner, c), :], wbuf.at[cg, :, owner_rows(owner, c), :],
            w_send.at[cg, 0, c], w_recv.at[cg, owner, c], dev_x,
        ).wait_recv()

    def w_forward(cg, c):
        owner, device = (rx, dev_y) if c % 2 == 0 else (ry, dev_x)
        return remote(
            wbuf.at[cg, :, owner_rows(owner, c), :], wbuf.at[cg, :, owner_rows(owner, c), :],
            w_fwd_send.at[cg, c], w_recv.at[cg, owner, c], device,
        )

    def w_go(cg, c):
        w_copy(cg, c, 0).start()
        w_copy(cg, c, 1).start()

    def w_step(cg, c):
        w_arrived(cg, rx, c)
        w_arrived(cg, ry, c)
        w_forward(cg, c).start()

    def pair_step(c):
        w_pair(c).wait_recv()
        w_go(1, c)

    grad_copy(0).start()

    @pl.when(middle)
    def _():
        go(x_pair, [0])
        go(x_mirror, every)
        go(x_stage, early)

    @pl.when(jnp.logical_not(middle))
    def _():
        go(x_pair, early)

    for i in range(1, len(order)):
        grad_copy(i).start()
    for g in range(GROUPS):
        x_swap(g).start()

    first_bias = 1.0 - 0.9**10
    second_bias = 1.0 - 0.95**10

    def adam(sub, c, out, base):
        def piece(i, carry):
            at = pl.ds(pl.multiple_of(sub * half + c * chunk + i * ADAM_SUB, ADAM_SUB), ADAM_SUB)
            gradient = own_grad[:, at, :].astype(jnp.float32) + peer_grad[:, at, :].astype(jnp.float32)
            new_one = 0.9 * one[:, at, :] + (1.0 - 0.9) * gradient
            new_two = 0.95 * two[:, at, :] + (1.0 - 0.95) * gradient * gradient
            update = new_one / first_bias / (jnp.sqrt(new_two / second_bias) + 1e-08)
            old = master[:, at, :]
            new_master = old - 0.001 * (update + 0.1 * old)
            one[:, at, :] = new_one
            two[:, at, :] = new_two
            master[:, at, :] = new_master
            to = pl.ds(pl.multiple_of(base + c * chunk + i * ADAM_SUB, ADAM_SUB), ADAM_SUB)
            out[:, to, :] = new_master.astype(jnp.bfloat16)
            return carry

        lax.fori_loop(0, chunk // ADAM_SUB, piece, 0)

    for i, (sub, c) in enumerate(order):
        grad_local[i].wait()
        for copy in state_local[i]:
            copy.wait()
        grad_copy(i).wait_recv()
        if i % 2 == 0:
            adam(sub, c, wpair, 0)
            w_pair(c).start()
        else:
            adam(sub, c, wbuf.at[0], r * half)
            if c < W_EARLY:
                w_go(0, c)

    outs = [
        pltpu.make_async_copy(master, master_out, out_sem.at[0]),
        pltpu.make_async_copy(one, one_out, out_sem.at[1]),
        pltpu.make_async_copy(two, two_out, out_sem.at[2]),
    ]
    for copy in outs:
        copy.start()
    x_local.wait()
    kv_local.wait()
    q_local.wait()
    length_local.wait()

    kv_rows, cache_len = kv_raw.shape[:2]
    parts = kv_rows // TAIL_ROWS
    head = HD
    groups = kv_raw.shape[3] // head
    per_group = q_raw.shape[2] // head // groups
    part_tokens = TAIL_ROWS * x_steps
    keys = TAIL_ROWS * cache_len
    column = lax.broadcasted_iota(jnp.int32, (1, keys), 1)
    key_row = column // cache_len
    position = column - key_row * cache_len
    token_row = lax.broadcasted_iota(jnp.int32, (part_tokens, 1), 0) // x_steps
    factor = head**-0.5 * LOG2E

    def cached_part(part):
        mine_rows = slice(part * TAIL_ROWS, (part + 1) * TAIL_ROWS)
        limit = jnp.zeros((1, keys), jnp.int32)
        for at in range(TAIL_ROWS):
            limit = jnp.where(key_row == at, lengths[part * TAIL_ROWS + at], limit)
        valid = jnp.where(position < limit, key_row, -1) == token_row
        for group in range(groups):
            cols = slice(group * head, (group + 1) * head)
            query = jnp.concatenate(
                [
                    q_raw[mine_rows, :, (group * per_group + h) * head : (group * per_group + h + 1) * head].reshape(
                        part_tokens, head
                    )
                    for h in range(per_group)
                ],
                axis=0,
            )
            key = kv_raw[mine_rows, :, 0, cols].reshape(keys, head)
            value = kv_raw[mine_rows, :, 1, cols].reshape(keys, head)
            scores = lax.dot_general(query, key, (((1,), (1,)), ((), ())), preferred_element_type=jnp.float32)
            scores = jnp.where(valid[None], scores.reshape(per_group, part_tokens, keys), LOW)
            scores = scores.reshape(per_group * part_tokens, keys)
            top = jnp.max(scores, axis=-1, keepdims=True)
            weights = jnp.exp2((scores - top) * factor)
            total = jnp.sum(weights, axis=-1, keepdims=True)
            old = jnp.dot(weights.astype(jnp.bfloat16), value, preferred_element_type=jnp.float32)
            where = part * groups + group
            query_out[where] = query
            old_out[where] = old * (1.0 / total)
            mass_out[where] = jnp.broadcast_to(top + jnp.log2(total) * (1.0 / factor), old.shape)

    @pl.when(middle)
    def _():
        for g in early:
            relay(g)

    @pl.when(jnp.logical_not(middle))
    def _():
        go(x_pair, late)

    def send_next(item):
        cg, c = item
        if cg == 1:
            pair_step(c)
        else:
            w_go(0, c)

    items = [(0, c) for c in range(W_EARLY)] + [(1, c) for c in range(W_CHUNKS)]
    items += [(0, c) for c in range(W_EARLY, W_CHUNKS)]
    for i in range(W_EARLY + W_CHUNKS):
        w_step(*items[i])
        if i + W_EARLY < len(items):
            send_next(items[i + W_EARLY])
            if items[i + W_EARLY] == (1, W_CHUNKS - 3):
                @pl.when(middle)
                def _():
                    go(x_pair, every[1:])

            if items[i + W_EARLY] == (1, W_CHUNKS - 2):
                @pl.when(middle)
                def _():
                    for g in early:
                        unstage(g)

                @pl.when(jnp.logical_not(middle))
                def _():
                    go(x_mirror, early)

            if items[i + W_EARLY] == (1, W_CHUNKS - 1):
                @pl.when(middle)
                def _():
                    for g in late:
                        relay(g)

            if items[i + W_EARLY] == (0, W_EARLY):
                @pl.when(middle)
                def _():
                    go(x_pair_mirror, late)

                @pl.when(jnp.logical_not(middle))
                def _():
                    go(x_mirror, late)

        if i < parts:
            cached_part(i)
    for part in range(W_EARLY + W_CHUNKS, parts):
        cached_part(part)
    for c in range(W_CHUNKS):
        w_arrived(1, rd, c)
    for c in range(W_EARLY):
        w_arrived(0, rd, c)
    for c in range(W_EARLY, W_CHUNKS - 1):
        w_step(0, c)

    def far_swap(g):
        return remote(
            far.at[nf, :, tokens(g), :], far_peer.at[:, tokens(g), :], far_send.at[g], far_recv.at[g], partner
        )

    def far_back(g):
        return remote(
            far_out.at[:, tokens(g), :], far_in.at[:, tokens(g), :], back_send.at[g], back_recv.at[g], (r, f, pair)
        )

    def near_part(lhs, kv, start, stop):
        total = None
        for k in range(blocks):
            at = slice(k * half + start * chunk, k * half + stop * chunk)
            product = jnp.dot(lhs[:, at], wbuf[0, kv, at, :], preferred_element_type=jnp.float32)
            total = product if total is None else total + product
        return total

    def far_step(g, carry):
        @pl.when(jnp.logical_not(middle))
        def _():
            for th in range(2):
                x_arrived(pair, th, g)

        x_arrived(t, nf, g)
        for th in range(2):
            x_arrived(mirror, th, g)
            x_arrived(pair_mirror, th, g)

        def flatten(k, inner):
            for th in range(2):
                piece = xbuf[k, th, pl.ds(g * group_rows, group_rows)].reshape(group_tokens, half)
                xflat[th, tokens(g), pl.ds(pl.multiple_of(k * half, half), half)] = piece
            return inner

        lax.fori_loop(0, blocks, flatten, 0)
        lhs = jnp.concatenate([xflat[0, tokens(g), :], xflat[1, tokens(g), :]], axis=0)
        for kv in range(2):
            product = jnp.dot(lhs, wbuf[1, kv], preferred_element_type=jnp.float32)
            for th in range(2):
                far[th, kv, tokens(g), :] = product[th * group_tokens : (th + 1) * group_tokens]
        far_swap(g).start()
        for kv in range(2):
            product = near_part(lhs, kv, 0, W_EARLY)
            for th in range(2):
                near[th, kv, tokens(g), :] = product[th * group_tokens : (th + 1) * group_tokens]
        return carry

    def far_done(g):
        far_swap(g).wait_recv()
        both = far[f, :, tokens(g), :] + far_peer[:, tokens(g), :]
        far_out[:, tokens(g), :] = both.astype(jnp.bfloat16)
        far_back(g).start()

    def far_loop(g, carry):
        far_step(g, 0)

        @pl.when(g > 0)
        def _():
            far_done(g - 1)

        @pl.when(g == 0)
        def _():
            w_step(0, W_CHUNKS - 1)

        return carry

    lax.fori_loop(0, GROUPS, far_loop, 0)
    far_done(GROUPS - 1)

    near_swap = remote(near.at[nf], near_peer, near_send.at[0], near_recv.at[0], partner)
    for c in range(W_EARLY, W_CHUNKS):
        w_arrived(0, rd, c)

    def near_last(i, carry):
        th = jnp.where(i == 0, nf, f)
        for kv in range(2):
            near[th, kv] += near_part(xflat.at[th], kv, W_EARLY, W_CHUNKS)

        @pl.when(i == 0)
        def _():
            near_swap.start()

        return carry

    lax.fori_loop(0, 2, near_last, 0)

    for i in range(len(order)):
        grad_copy(i).wait_send()
    for c in range(W_CHUNKS):
        w_pair(c).wait_send()
        for cg in range(2):
            w_copy(cg, c, 0).wait_send()
            w_copy(cg, c, 1).wait_send()
            w_forward(cg, c).wait_send()
    for g in range(GROUPS):
        x_swap(g).wait_send()
        for h in range(2):
            x_pair(g, h).wait_send()
            x_mirror(g, h).wait_send()
        far_swap(g).wait_send()
        far_back(g).wait_send()

    @pl.when(middle)
    def _():
        for h in range(2):
            for g in every:
                x_relay(g, h).wait_send()
            for g in early:
                x_stage(g, h).wait_send()
                x_unstage(g, h).wait_send()
            for g in late:
                x_pair_mirror(g, h).wait_send()

    for copy in outs:
        copy.wait()
    for g in range(GROUPS):
        far_back(g).wait_recv()
    near_swap.wait_recv()
    fresh_out[...] = (near[f] + near_peer[...] + far_in[...].astype(jnp.float32)).astype(jnp.bfloat16)
    near_swap.wait_send()


def tail_kernel(
    query_ref, old_ref, mass_ref, fresh_ref, master_in, one_in, two_in,
    context, master_out, one_out, two_out, out_ref, sem,
):
    moves = [
        pltpu.make_async_copy(source.at[kv], target.at[kv], sem.at[2 * i + kv])
        for i, (source, target) in enumerate(((master_in, master_out), (one_in, one_out), (two_in, two_out)))
        for kv in range(2)
    ]
    for move in moves:
        move.start()
    row_count, step_count, features = out_ref.shape
    head = HD
    groups = fresh_ref.shape[2] // head
    per_group = features // head // groups
    tokens = TAIL_ROWS * step_count
    parts = row_count // TAIL_ROWS
    token = lax.broadcasted_iota(jnp.int32, (tokens, 1), 0)
    column = lax.broadcasted_iota(jnp.int32, (1, tokens), 1)
    valid = (column // step_count == token // step_count) & (column <= token)
    factor = head**-0.5 * LOG2E
    contract = (((1,), (1,)), ((), ()))
    writes = []
    for part in range(parts):
        here = slice(part * tokens, (part + 1) * tokens)
        mine = slice(part * TAIL_ROWS, (part + 1) * TAIL_ROWS)
        for group in range(groups):
            cols = slice(group * head, (group + 1) * head)
            where = part * groups + group
            scores = lax.dot_general(
                query_ref[where], fresh_ref[0, here, cols], contract, preferred_element_type=jnp.float32
            )
            scores = jnp.where(valid[None], scores.reshape(per_group, tokens, tokens), LOW)
            scores = scores.reshape(per_group * tokens, tokens)
            mass = mass_ref[where]
            top = jnp.maximum(mass, jnp.max(scores, axis=-1, keepdims=True))
            old_weight = jnp.exp2((mass - top) * factor)
            weights = jnp.exp2((scores - top[:, :tokens]) * factor)
            scale = 1.0 / (old_weight + jnp.sum(weights, axis=-1, keepdims=True))
            new = jnp.dot(weights.astype(jnp.bfloat16), fresh_ref[1, here, cols], preferred_element_type=jnp.float32)
            out = (old_weight * old_ref[where] + new) * scale
            for h in range(per_group):
                at = (group * per_group + h) * head
                piece = out[h * tokens : (h + 1) * tokens].reshape(TAIL_ROWS, step_count, head)
                out_ref[mine, :, at : at + head] = piece.astype(jnp.bfloat16)
        write = pltpu.make_async_copy(out_ref.at[mine], context.at[mine], sem.at[6 + part])
        write.start()
        writes.append(write)
    for write in writes + moves:
        write.wait()


def fused_device(n_rep, grad_parts, master_weight, moment_one, moment_two, layer_inputs, queries, kv_cache, lengths):
    row_count, step_count, features = layer_inputs.shape
    _, depth, width = master_weight.shape
    n_tp = n_rep
    tokens = row_count * step_count
    bf16, f32 = jnp.bfloat16, jnp.float32
    dma = pltpu.SemaphoreType.DMA
    state = jax.ShapeDtypeStruct(master_weight.shape, f32)
    any_spec = pl.BlockSpec(memory_space=pl.ANY)
    hbm_spec = pl.BlockSpec(memory_space=pltpu.HBM)
    in_place = [
        pltpu.with_memory_space_constraint(array, pltpu.HBM)
        for array in (lengths, grad_parts, master_weight, moment_one, moment_two, layer_inputs, kv_cache, queries)
    ]
    half = depth // 2
    vmem_spec = pl.BlockSpec(memory_space=pltpu.VMEM)
    parts = row_count // TAIL_ROWS
    groups = width // HD
    stacked = (parts * groups, queries.shape[2] // width * TAIL_ROWS * step_count, HD)
    fresh, query, old, mass, master, one, two = pl.pallas_call(
        learner_kernel,
        out_shape=(
            jax.ShapeDtypeStruct((2, tokens, width), bf16),
            jax.ShapeDtypeStruct(stacked, bf16),
            jax.ShapeDtypeStruct(stacked, f32),
            jax.ShapeDtypeStruct(stacked, f32),
            state,
            state,
            state,
        ),
        in_specs=[hbm_spec] * 8,
        out_specs=(vmem_spec,) * 4 + (any_spec,) * 3,
        scratch_shapes=[
            pltpu.VMEM((2, depth, width), bf16),
            pltpu.VMEM((2, depth, width), bf16),
            pltpu.VMEM((2, depth, width), f32),
            pltpu.VMEM((2, depth, width), f32),
            pltpu.VMEM((2, depth, width), f32),
            pltpu.VMEM((2, half, width), bf16),
            pltpu.VMEM((2, 2, n_rep * half, width), bf16),
            pltpu.VMEM((n_tp, 2, row_count, step_count, half), bf16),
            pltpu.VMEM((2, tokens, n_tp * half), bf16),
            pltpu.VMEM((2, 2, tokens, width), f32),
            pltpu.VMEM((2, tokens, width), f32),
            pltpu.VMEM((2, tokens, width), bf16),
            pltpu.VMEM((2, tokens, width), bf16),
            pltpu.VMEM((2, 2, tokens, width), f32),
            pltpu.VMEM((2, tokens, width), f32),
            pltpu.VMEM(kv_cache.shape, bf16),
            pltpu.VMEM(queries.shape, bf16),
            pltpu.SMEM(lengths.shape, jnp.int32),
            pltpu.VMEM((2, row_count, step_count, half), bf16),
            dma((2 * W_CHUNKS,)),
            dma((3, 2 * W_CHUNKS)),
            dma((1,)),
            dma((3,)),
            dma((3,)),
            dma((2 * W_CHUNKS,)),
            dma((2 * W_CHUNKS,)),
            dma((9, GROUPS)),
            dma((n_tp, 2, GROUPS)),
            dma((2, GROUPS)),
            dma((2, GROUPS)),
            dma((W_CHUNKS,)),
            dma((W_CHUNKS,)),
            dma((2, 2, W_CHUNKS)),
            dma((2, n_rep, W_CHUNKS)),
            dma((2, W_CHUNKS)),
            dma((GROUPS,)),
            dma((GROUPS,)),
            dma((GROUPS,)),
            dma((GROUPS,)),
            dma((1,)),
            dma((1,)),
        ],
        compiler_params=pltpu.CompilerParams(
            collective_id=0, has_side_effects=True, vmem_limit_bytes=36 * 1024 * 1024
        ),
    )(*in_place)
    context, master, one, two = pl.pallas_call(
        tail_kernel,
        out_shape=(jax.ShapeDtypeStruct(queries.shape, bf16), state, state, state),
        in_specs=[vmem_spec] * 4 + [any_spec] * 3,
        out_specs=(hbm_spec,) * 4,
        scratch_shapes=[pltpu.VMEM(queries.shape, bf16), dma((6 + parts,))],
        compiler_params=pltpu.CompilerParams(vmem_limit_bytes=16 * 1024 * 1024),
    )(query, old, mass, fresh, master, one, two)
    return (master, one, two, context)


beta_one = 0.9
beta_two = 0.95
learning_rate = 0.001
weight_decay = 0.1
epsilon = 1e-08
first_bias = 1.0 - 0.9**10
second_bias = 1.0 - 0.95**10


def adamw_update(gradient, master, moment_one, moment_two):
    new_one = beta_one * moment_one + (1.0 - beta_one) * gradient
    new_two = beta_two * moment_two + (1.0 - beta_two) * gradient * gradient
    update = new_one / first_bias / (jnp.sqrt(new_two / second_bias) + epsilon)
    new_master = master - learning_rate * (update + weight_decay * master)
    return (new_one, new_two, new_master)


def attend(queries, kv_cache, fresh_keys, fresh_values, lengths):
    row_count = queries.shape[0]
    step_count = queries.shape[1]
    kv_heads = fresh_keys.shape[2]
    cache_len = kv_cache.shape[1]
    grouped = queries.reshape(row_count, step_count, kv_heads, -1, HD)
    cached_keys = kv_cache[:, :, 0].reshape(row_count, cache_len, kv_heads, HD)
    cached_values = kv_cache[:, :, 1].reshape(row_count, cache_len, kv_heads, HD)
    scaling = 1.0 / jnp.sqrt(jnp.float32(HD))
    cached_scores = (
        jnp.einsum("rsgqd,rcgd->rsgqc", grouped, cached_keys, preferred_element_type=jnp.float32)
        * scaling
    )
    fresh_scores = (
        jnp.einsum("rsgqd,rugd->rsgqu", grouped, fresh_keys, preferred_element_type=jnp.float32)
        * scaling
    )
    valid_old = jnp.arange(cache_len, dtype=jnp.int32)[None, :] < lengths[:, None]
    valid_old = valid_old[:, None, None, None, :]
    steps_index = jnp.arange(step_count, dtype=jnp.int32)
    valid_new = (steps_index[None, :] <= steps_index[:, None])[None, :, None, None, :]
    scores = jnp.concatenate(
        [
            jnp.where(valid_old, cached_scores, -jnp.inf),
            jnp.where(valid_new, fresh_scores, -jnp.inf),
        ],
        axis=-1,
    )
    row_max = jnp.max(scores, axis=-1, keepdims=True)
    exponent = jnp.exp(scores - row_max)
    weights = (exponent / jnp.sum(exponent, axis=-1, keepdims=True)).astype(jnp.bfloat16)
    output = jnp.einsum(
        "rsgqc,rcgd->rsgqd",
        weights[..., :cache_len],
        cached_values,
        preferred_element_type=jnp.float32,
    )
    output = output + jnp.einsum(
        "rsgqu,rugd->rsgqd",
        weights[..., cache_len:],
        fresh_values,
        preferred_element_type=jnp.float32,
    )
    return output.astype(jnp.bfloat16).reshape(row_count, step_count, -1)


def on_device(
    grad_parts, master_weight, moment_one, moment_two, layer_inputs, queries, kv_cache, lengths
):
    gradient = lax.psum_scatter(
        grad_parts[0].astype(jnp.float32).astype(jnp.bfloat16),
        "fsdp",
        scatter_dimension=1,
        tiled=True,
    ).astype(jnp.float32)
    new_one, new_two, new_master = adamw_update(gradient, master_weight, moment_one, moment_two)
    rollout_weight = new_master.astype(jnp.bfloat16)
    row_count = layer_inputs.shape[0]
    step_count = layer_inputs.shape[1]
    gathered = lax.all_gather(layer_inputs, "tp", axis=2, tiled=True)
    flattened = gathered.reshape(row_count * step_count, gathered.shape[2])
    projected = jnp.einsum(
        "td,kdc->ktc",
        flattened,
        lax.all_gather(rollout_weight, ("rep", "fsdp"), axis=1, tiled=True),
        preferred_element_type=jnp.float32,
    )
    fresh_pair = projected.astype(jnp.bfloat16).reshape(2, row_count, step_count, -1, HD)
    context = attend(queries, kv_cache, fresh_pair[0], fresh_pair[1], lengths)
    return (new_master, new_one, new_two, context)


def solution(mesh):
    shape = mesh.shape
    fits = shape["rep"] == 4 and shape["tp"] == 4 and shape["fsdp"] == 2
    run = functools.partial(fused_device, shape["rep"]) if fits else on_device
    return jax.shard_map(
        run,
        mesh=mesh,
        in_specs=(
            P("fsdp", None, "rep", "tp"),
            P(None, ("rep", "fsdp"), "tp"),
            P(None, ("rep", "fsdp"), "tp"),
            P(None, ("rep", "fsdp"), "tp"),
            P(("rep", "fsdp"), None, "tp"),
            P(("rep", "fsdp"), None, "tp"),
            P(("rep", "fsdp"), None, None, "tp"),
            P(("rep", "fsdp")),
        ),
        out_specs=(
            P(None, ("rep", "fsdp"), "tp"),
            P(None, ("rep", "fsdp"), "tp"),
            P(None, ("rep", "fsdp"), "tp"),
            P(("rep", "fsdp"), None, "tp"),
        ),
        check_vma=False,
    )
```

```python
import functools

import jax
import jax.numpy as jnp
from jax import lax
from jax.experimental import pallas as pl
from jax.experimental.pallas import tpu as pltpu
from jax.sharding import PartitionSpec as P

HD = 128
MESH = pl.DeviceIdType.MESH
W_CHUNKS = 4
W_EARLY = 2
GROUPS = 2
ADAM_SUB = 32
TAIL_ROWS = 8
LOG2E = 1.4426950408889634
LOW = -0.7 * 3.4028234663852886e38


def learner_kernel(
    lengths_hbm, grad_hbm, master_hbm, one_hbm, two_hbm, x_hbm, kv_hbm, q_hbm,
    fresh_out, query_out, old_out, mass_out, master_out, one_out, two_out,
    own_grad, peer_grad, master, one, two, wpair, wbuf, xbuf, xstage, xflat,
    far, far_peer, far_out, far_in, near, near_peer, kv_raw, q_raw, lengths,
    state_sem, local_sem, out_sem, grad_send, grad_recv, x_send, x_recv, stage_recv,
    pair_send, pair_recv, w_send, w_near, w_diag, far_send, far_recv, back_send, back_recv, near_send, near_recv,
):
    r, f, t = lax.axis_index("rep"), lax.axis_index("fsdp"), lax.axis_index("tp")
    nf = 1 - f
    rx = r + 1 - 2 * lax.rem(r, 2)
    ry = lax.rem(r + 2, 4)
    rd = lax.rem(rx + 2, 4)
    partner, dev_x, dev_y = (r, nf, t), (rx, f, t), (ry, f, t)
    pair = t + 1 - 2 * lax.rem(t, 2)
    mirror = 3 - t
    pair_mirror = 3 - pair
    middle = (t == 1) | (t == 2)
    mine = lax.rem((t + 1) // 2, 2)
    theirs = 1 - mine
    depth = master.shape[1]
    half = depth // 2
    chunk = half // W_CHUNKS
    x_rows, x_steps = xbuf.shape[2:4]
    group_rows = x_rows // GROUPS
    group_tokens = group_rows * x_steps
    blocks = wbuf.shape[2] // half

    def state_rows(sub, c):
        return pl.ds(pl.multiple_of(sub * half + c * chunk, chunk), chunk)

    def owner_rows(owner, c):
        return pl.ds(pl.multiple_of(owner * half + c * chunk, chunk), chunk)

    order = []
    for c in range(W_CHUNKS):
        order += [(mine, c), (theirs, c)]

    def features(h, sub):
        return pl.ds(pl.multiple_of(h * depth + sub * half, half), half)

    def some_rows(g):
        return pl.ds(g * group_rows, group_rows)

    def tokens(g):
        return pl.ds(g * group_tokens, group_tokens)

    state_local = []
    for i, sub in enumerate((mine, theirs)):
        at = pl.ds(pl.multiple_of(sub * half, half), half)
        source = pl.ds(pl.multiple_of(f * depth + sub * half, half), half)
        state_local.append([
            pltpu.make_async_copy(hbm, vmem, state_sem.at[j, i])
            for j, (hbm, vmem) in enumerate((
                (grad_hbm.at[0, :, source, :], own_grad.at[:, at, :]),
                (master_hbm.at[:, at, :], master.at[:, at, :]),
                (one_hbm.at[:, at, :], one.at[:, at, :]),
                (two_hbm.at[:, at, :], two.at[:, at, :]),
            ))
        ])
        for copy in state_local[i]:
            copy.start()
    local = [
        pltpu.make_async_copy(x_hbm.at[:, :, features(f, mine)], xbuf.at[t, f], local_sem.at[0]),
        pltpu.make_async_copy(kv_hbm, kv_raw, local_sem.at[1]),
        pltpu.make_async_copy(q_hbm, q_raw, local_sem.at[2]),
        pltpu.make_async_copy(lengths_hbm, lengths, local_sem.at[3]),
    ]
    for copy in local:
        copy.start()

    barrier = pltpu.get_barrier_semaphore()
    friends = [partner, dev_x, dev_y]
    for i in range(1, blocks):
        for h in range(2):
            friends.append((r, h, lax.rem(t + i, blocks)))
    for device in friends:
        pl.semaphore_signal(barrier, inc=1, device_id=device, device_id_type=MESH)
    pl.semaphore_wait(barrier, len(friends))

    def remote(src, dst, send, recv, device):
        return pltpu.make_async_remote_copy(
            src_ref=src, dst_ref=dst, send_sem=send, recv_sem=recv,
            device_id=device, device_id_type=MESH,
        )

    def drain(ref, sem):
        remote(ref, ref, sem, sem, partner).wait_send()

    def landed(ref, sem):
        remote(ref, ref, sem, sem, partner).wait_recv()

    def grad_copy(i):
        sub, c = order[i]
        source = pl.ds(pl.multiple_of(nf * depth + sub * half + c * chunk, chunk), chunk)
        return remote(
            grad_hbm.at[0, :, source, :], peer_grad.at[:, state_rows(sub, c), :],
            grad_send.at[0], grad_recv.at[i], partner,
        )

    def x_own(g, h, sub, slot, device):
        remote(
            x_hbm.at[some_rows(g), :, features(h, sub)], xbuf.at[t, f, some_rows(g)],
            x_send.at[slot], x_recv.at[t, g], device,
        ).start()

    def x_swap(g):
        x_own(g, nf, mine, 0, partner)

    def x_mirror(g):
        for h in range(2):
            x_own(g, h, mine, 1, (r, h, mirror))

    def x_pair(g, h):
        x_own(g, h, theirs, 2, (r, h, pair))

    def x_pair_mirror(g):
        for h in range(2):
            x_own(g, h, theirs, 3, (r, h, pair_mirror))

    def x_arrived(k, g):
        landed(xbuf.at[k, :, some_rows(g)], x_recv.at[k, g])

    def relay(g):
        x_arrived(pair, g)
        remote(
            xbuf.at[pair, :, some_rows(g)], xbuf.at[pair, :, some_rows(g)],
            x_send.at[4], x_recv.at[pair, g], (r, f, mirror),
        ).start()

    def x_stage(h):
        remote(
            x_hbm.at[some_rows(0), :, features(h, theirs)], xstage.at[f],
            x_send.at[3], stage_recv.at[0], (r, h, mirror),
        ).start()

    def unstage():
        landed(xstage, stage_recv.at[0])
        remote(
            xstage, xbuf.at[mirror, :, some_rows(0)], x_send.at[5], x_recv.at[mirror, 0], (r, f, pair)
        ).start()

    def w_pair(c):
        return remote(
            wpair.at[:, pl.ds(c * chunk, chunk), :], wbuf.at[1, :, owner_rows(r, c), :],
            pair_send.at[0], pair_recv.at[c], (r, f, pair),
        )

    def w_go(cg, c):
        at = wbuf.at[cg, :, owner_rows(r, c), :]
        remote(at, at, w_send.at[0], w_near.at[cg, c], dev_x).start()
        remote(at, at, w_send.at[1], w_near.at[cg, c], dev_y).start()

    def w_step(cg, c):
        landed(wbuf.at[cg, :, pl.ds(0, 2 * chunk), :], w_near.at[cg, c])
        owner, device = (rx, dev_y) if c % 2 == 0 else (ry, dev_x)
        at = wbuf.at[cg, :, owner_rows(owner, c), :]
        remote(at, at, w_send.at[2], w_diag.at[cg, c], device).start()

    def w_last(cg, c):
        landed(wbuf.at[cg, :, owner_rows(rd, c), :], w_diag.at[cg, c])

    def pair_step(c):
        w_pair(c).wait_recv()
        w_go(1, c)

    grad_copy(0).start()

    @pl.when(middle)
    def _():
        x_pair(0, 0)
        x_mirror(0)
        x_mirror(1)
        x_stage(0)
        x_stage(1)

    @pl.when(jnp.logical_not(middle))
    def _():
        x_pair(0, 0)
        x_pair(0, 1)

    for i in range(1, len(order)):
        grad_copy(i).start()
    for g in range(GROUPS):
        x_swap(g)

    first_bias = 1.0 - 0.9**10
    second_bias = 1.0 - 0.95**10

    def adam(sub, c, out, base):
        def piece(i, carry):
            at = pl.ds(pl.multiple_of(sub * half + c * chunk + i * ADAM_SUB, ADAM_SUB), ADAM_SUB)
            gradient = own_grad[:, at, :].astype(jnp.float32) + peer_grad[:, at, :].astype(jnp.float32)
            new_one = 0.9 * one[:, at, :] + (1.0 - 0.9) * gradient
            new_two = 0.95 * two[:, at, :] + (1.0 - 0.95) * gradient * gradient
            update = new_one / first_bias / (jnp.sqrt(new_two / second_bias) + 1e-08)
            old = master[:, at, :]
            new_master = old - 0.001 * (update + 0.1 * old)
            one[:, at, :] = new_one
            two[:, at, :] = new_two
            master[:, at, :] = new_master
            to = pl.ds(pl.multiple_of(base + c * chunk + i * ADAM_SUB, ADAM_SUB), ADAM_SUB)
            out[:, to, :] = new_master.astype(jnp.bfloat16)
            return carry

        lax.fori_loop(0, chunk // ADAM_SUB, piece, 0)

    for i, (sub, c) in enumerate(order):
        if i < 2:
            for copy in state_local[i]:
                copy.wait()
        grad_copy(i).wait_recv()
        if i % 2 == 1:
            adam(sub, c, wpair, 0)
            w_pair(c).start()
        else:
            adam(sub, c, wbuf.at[0], r * half)
            if c < W_EARLY:
                w_go(0, c)
    outs = [
        pltpu.make_async_copy(master, master_out, out_sem.at[0]),
        pltpu.make_async_copy(one, one_out, out_sem.at[1]),
        pltpu.make_async_copy(two, two_out, out_sem.at[2]),
    ]
    for copy in outs:
        copy.start()
    for copy in local:
        copy.wait()

    kv_rows, cache_len = kv_raw.shape[:2]
    parts = kv_rows // TAIL_ROWS
    head = HD
    groups = kv_raw.shape[3] // head
    per_group = q_raw.shape[2] // head // groups
    part_tokens = TAIL_ROWS * x_steps
    keys = TAIL_ROWS * cache_len
    column = lax.broadcasted_iota(jnp.int32, (1, keys), 1)
    key_row = column // cache_len
    position = column - key_row * cache_len
    token_row = lax.broadcasted_iota(jnp.int32, (part_tokens, 1), 0) // x_steps
    factor = head**-0.5 * LOG2E

    def cached_part(part):
        mine_rows = slice(part * TAIL_ROWS, (part + 1) * TAIL_ROWS)
        limit = jnp.zeros((1, keys), jnp.int32)
        for at in range(TAIL_ROWS):
            limit = jnp.where(key_row == at, lengths[part * TAIL_ROWS + at], limit)
        valid = jnp.where(position < limit, key_row, -1) == token_row
        for group in range(groups):
            cols = slice(group * head, (group + 1) * head)
            query = jnp.concatenate(
                [
                    q_raw[mine_rows, :, (group * per_group + h) * head : (group * per_group + h + 1) * head].reshape(
                        part_tokens, head
                    )
                    for h in range(per_group)
                ],
                axis=0,
            )
            key = kv_raw[mine_rows, :, 0, cols].reshape(keys, head)
            value = kv_raw[mine_rows, :, 1, cols].reshape(keys, head)
            scores = lax.dot_general(query, key, (((1,), (1,)), ((), ())), preferred_element_type=jnp.float32)
            scores = jnp.where(valid[None], scores.reshape(per_group, part_tokens, keys), LOW)
            scores = scores.reshape(per_group * part_tokens, keys)
            top = jnp.max(scores, axis=-1, keepdims=True)
            weights = jnp.exp2((scores - top) * factor)
            total = jnp.sum(weights, axis=-1, keepdims=True)
            old = jnp.dot(weights.astype(jnp.bfloat16), value, preferred_element_type=jnp.float32)
            where = part * groups + group
            query_out[where] = query
            old_out[where] = old * (1.0 / total)
            mass_out[where] = jnp.broadcast_to(top + jnp.log2(total) * (1.0 / factor), old.shape)

    @pl.when(middle)
    def _():
        relay(0)

    @pl.when(jnp.logical_not(middle))
    def _():
        x_pair(1, 0)
        x_pair(1, 1)

    def send_next(item):
        cg, c = item
        if cg == 1:
            pair_step(c)
        else:
            w_go(0, c)

    items = [(0, c) for c in range(W_EARLY)] + [(1, c) for c in range(W_CHUNKS)]
    items += [(0, c) for c in range(W_EARLY, W_CHUNKS)]
    for c in range(W_EARLY):
        w_step(0, c)
    for i in range(W_EARLY + W_CHUNKS):
        if i >= W_EARLY:
            w_step(*items[i])
        upcoming = items[i + W_EARLY]
        send_next(upcoming)
        if upcoming == (1, W_CHUNKS - 3):
            @pl.when(middle)
            def _():
                x_pair(0, 1)

        if upcoming == (1, W_CHUNKS - 2):
            @pl.when(middle)
            def _():
                unstage()
                relay(1)

            @pl.when(jnp.logical_not(middle))
            def _():
                x_mirror(0)

        if upcoming == (1, W_CHUNKS - 1):
            @pl.when(middle)
            def _():
                x_pair(1, 0)
                x_pair(1, 1)

        if upcoming == (0, W_EARLY):
            @pl.when(middle)
            def _():
                x_pair_mirror(1)

            @pl.when(jnp.logical_not(middle))
            def _():
                x_mirror(1)

        if i < parts:
            cached_part(i)
    for part in range(W_EARLY + W_CHUNKS, parts):
        cached_part(part)

    def far_swap(g):
        return remote(
            far.at[nf, :, tokens(g), :], far_peer.at[:, tokens(g), :], far_send.at[0], far_recv.at[g], partner
        )

    def far_back(g):
        return remote(
            far_out.at[:, tokens(g), :], far_in.at[:, tokens(g), :], back_send.at[0], back_recv.at[g], (r, f, pair)
        )

    def near_swap(g):
        return remote(
            near.at[nf, :, tokens(g), :], near_peer.at[:, tokens(g), :], near_send.at[0], near_recv.at[g], partner
        )

    def flatten(g):
        def one_block(k, carry):
            for th in range(2):
                piece = xbuf[k, th, some_rows(g)].reshape(group_tokens, half)
                xflat[g, pl.ds(th * group_tokens, group_tokens), pl.ds(pl.multiple_of(k * half, half), half)] = piece
            return carry

        lax.fori_loop(0, blocks, one_block, 0)

    def multiply(cg, out, g, start, stop):
        for kv in range(2):
            total = None
            if stop - start == W_CHUNKS:
                total = jnp.dot(xflat[g], wbuf[cg, kv], preferred_element_type=jnp.float32)
            else:
                for k in range(blocks):
                    at = slice(k * half + start * chunk, k * half + stop * chunk)
                    product = jnp.dot(xflat[g, :, at], wbuf[cg, kv, at, :], preferred_element_type=jnp.float32)
                    total = product if total is None else total + product
            for th in range(2):
                piece = total[th * group_tokens : (th + 1) * group_tokens]
                if start > 0:
                    out[th, kv, tokens(g), :] += piece
                else:
                    out[th, kv, tokens(g), :] = piece

    def far_done(g):
        far_swap(g).wait_recv()
        both = far[f, :, tokens(g), :] + far_peer[:, tokens(g), :]
        far_out[:, tokens(g), :] = both.astype(jnp.bfloat16)
        far_back(g).start()

    def x_ready(g):
        landed(xbuf.at[t, nf, some_rows(g)], x_recv.at[t, g])
        x_arrived(mirror, g)
        x_arrived(pair_mirror, g)
        flatten(g)

    for c in range(W_EARLY):
        w_last(0, c)
        w_last(1, c)

    @pl.when(jnp.logical_not(middle))
    def _():
        x_arrived(pair, 0)

    x_ready(0)
    multiply(1, far, 0, 0, W_EARLY)
    multiply(0, near, 0, 0, W_EARLY)

    for c in range(W_EARLY, W_CHUNKS - 1):
        w_step(0, c)

    @pl.when(middle)
    def _():
        x_ready(1)
        multiply(1, far, 1, 0, W_EARLY)

    for c in range(W_EARLY, W_CHUNKS):
        w_last(1, c)
    multiply(1, far, 0, W_EARLY, W_CHUNKS)
    far_swap(0).start()

    @pl.when(middle)
    def _():
        multiply(1, far, 1, W_EARLY, W_CHUNKS)
        far_swap(1).start()

    far_done(0)
    w_step(0, W_CHUNKS - 1)

    @pl.when(jnp.logical_not(middle))
    def _():
        x_arrived(pair, 1)
        x_ready(1)
        multiply(1, far, 1, 0, W_CHUNKS)
        far_swap(1).start()

    @pl.when(middle)
    def _():
        far_done(1)

    multiply(0, near, 1, 0, W_EARLY)

    @pl.when(jnp.logical_not(middle))
    def _():
        far_done(1)

    for c in range(W_EARLY, W_CHUNKS):
        w_last(0, c)
    for g in range(GROUPS):
        multiply(0, near, g, W_EARLY, W_CHUNKS)
        near_swap(g).start()

    drain(peer_grad, grad_send.at[0])
    drain(xbuf.at[0, 0], x_send.at[0])
    drain(xbuf.at[0], x_send.at[1])
    drain(xbuf.at[0], x_send.at[2])

    @pl.when(middle)
    def _():
        drain(xbuf.at[0], x_send.at[3])
        drain(xbuf.at[0], x_send.at[4])
        drain(xstage, x_send.at[5])

    drain(wpair, pair_send.at[0])
    for way in range(3):
        drain(wbuf.at[:, :, pl.ds(0, half), :], w_send.at[way])
    drain(far.at[0], far_send.at[0])
    drain(far_out, back_send.at[0])
    for copy in outs:
        copy.wait()
    for g in range(GROUPS):
        near_swap(g).wait_recv()
    for g in range(GROUPS):
        far_back(g).wait_recv()
    fresh_out[...] = (near[f] + near_peer[...] + far_in[...].astype(jnp.float32)).astype(jnp.bfloat16)
    drain(near.at[0], near_send.at[0])


def tail_kernel(
    query_ref, old_ref, mass_ref, fresh_ref, master_in, one_in, two_in,
    context, master_out, one_out, two_out, out_ref, sem,
):
    moves = [
        pltpu.make_async_copy(source.at[kv], target.at[kv], sem.at[2 * i + kv])
        for i, (source, target) in enumerate(((master_in, master_out), (one_in, one_out), (two_in, two_out)))
        for kv in range(2)
    ]
    for move in moves:
        move.start()
    row_count, step_count, features = out_ref.shape
    head = HD
    groups = fresh_ref.shape[2] // head
    per_group = features // head // groups
    tokens = TAIL_ROWS * step_count
    parts = row_count // TAIL_ROWS
    token = lax.broadcasted_iota(jnp.int32, (tokens, 1), 0)
    column = lax.broadcasted_iota(jnp.int32, (1, tokens), 1)
    valid = (column // step_count == token // step_count) & (column <= token)
    factor = head**-0.5 * LOG2E
    contract = (((1,), (1,)), ((), ()))
    writes = []
    for part in range(parts):
        here = slice(part * tokens, (part + 1) * tokens)
        mine = slice(part * TAIL_ROWS, (part + 1) * TAIL_ROWS)
        for group in range(groups):
            cols = slice(group * head, (group + 1) * head)
            where = part * groups + group
            scores = lax.dot_general(
                query_ref[where], fresh_ref[0, here, cols], contract, preferred_element_type=jnp.float32
            )
            scores = jnp.where(valid[None], scores.reshape(per_group, tokens, tokens), LOW)
            scores = scores.reshape(per_group * tokens, tokens)
            mass = mass_ref[where]
            top = jnp.maximum(mass, jnp.max(scores, axis=-1, keepdims=True))
            old_weight = jnp.exp2((mass - top) * factor)
            weights = jnp.exp2((scores - top[:, :tokens]) * factor)
            scale = 1.0 / (old_weight + jnp.sum(weights, axis=-1, keepdims=True))
            new = jnp.dot(weights.astype(jnp.bfloat16), fresh_ref[1, here, cols], preferred_element_type=jnp.float32)
            out = (old_weight * old_ref[where] + new) * scale
            for h in range(per_group):
                at = (group * per_group + h) * head
                piece = out[h * tokens : (h + 1) * tokens].reshape(TAIL_ROWS, step_count, head)
                out_ref[mine, :, at : at + head] = piece.astype(jnp.bfloat16)
        write = pltpu.make_async_copy(out_ref.at[mine], context.at[mine], sem.at[6 + part])
        write.start()
        writes.append(write)
    for write in writes + moves:
        write.wait()


def fused_device(n_rep, grad_parts, master_weight, moment_one, moment_two, layer_inputs, queries, kv_cache, lengths):
    row_count, step_count, features = layer_inputs.shape
    _, depth, width = master_weight.shape
    n_tp = n_rep
    tokens = row_count * step_count
    bf16, f32 = jnp.bfloat16, jnp.float32
    dma = pltpu.SemaphoreType.DMA
    state = jax.ShapeDtypeStruct(master_weight.shape, f32)
    any_spec = pl.BlockSpec(memory_space=pl.ANY)
    hbm_spec = pl.BlockSpec(memory_space=pltpu.HBM)
    in_place = [
        pltpu.with_memory_space_constraint(array, pltpu.HBM)
        for array in (lengths, grad_parts, master_weight, moment_one, moment_two, layer_inputs, kv_cache, queries)
    ]
    half = depth // 2
    vmem_spec = pl.BlockSpec(memory_space=pltpu.VMEM)
    parts = row_count // TAIL_ROWS
    groups = width // HD
    stacked = (parts * groups, queries.shape[2] // width * TAIL_ROWS * step_count, HD)
    fresh, query, old, mass, master, one, two = pl.pallas_call(
        learner_kernel,
        out_shape=(
            jax.ShapeDtypeStruct((2, tokens, width), bf16),
            jax.ShapeDtypeStruct(stacked, bf16),
            jax.ShapeDtypeStruct(stacked, f32),
            jax.ShapeDtypeStruct(stacked, f32),
            state,
            state,
            state,
        ),
        in_specs=[hbm_spec] * 8,
        out_specs=(vmem_spec,) * 4 + (any_spec,) * 3,
        scratch_shapes=[
            pltpu.VMEM((2, depth, width), bf16),
            pltpu.VMEM((2, depth, width), bf16),
            pltpu.VMEM((2, depth, width), f32),
            pltpu.VMEM((2, depth, width), f32),
            pltpu.VMEM((2, depth, width), f32),
            pltpu.VMEM((2, half, width), bf16),
            pltpu.VMEM((2, 2, n_rep * half, width), bf16),
            pltpu.VMEM((n_tp, 2, row_count, step_count, half), bf16),
            pltpu.VMEM((2, row_count // GROUPS, step_count, half), bf16),
            pltpu.VMEM((GROUPS, 2 * tokens // GROUPS, n_tp * half), bf16),
            pltpu.VMEM((2, 2, tokens, width), f32),
            pltpu.VMEM((2, tokens, width), f32),
            pltpu.VMEM((2, tokens, width), bf16),
            pltpu.VMEM((2, tokens, width), bf16),
            pltpu.VMEM((2, 2, tokens, width), f32),
            pltpu.VMEM((2, tokens, width), f32),
            pltpu.VMEM(kv_cache.shape, bf16),
            pltpu.VMEM(queries.shape, bf16),
            pltpu.SMEM(lengths.shape, jnp.int32),
            dma((4, 2)),
            dma((4,)),
            dma((3,)),
            dma((1,)),
            dma((2 * W_CHUNKS,)),
            dma((6,)),
            dma((n_tp, GROUPS)),
            dma((1,)),
            dma((1,)),
            dma((W_CHUNKS,)),
            dma((3,)),
            dma((2, W_CHUNKS)),
            dma((2, W_CHUNKS)),
            dma((1,)),
            dma((GROUPS,)),
            dma((1,)),
            dma((GROUPS,)),
            dma((1,)),
            dma((GROUPS,)),
        ],
        compiler_params=pltpu.CompilerParams(
            collective_id=0, has_side_effects=True, vmem_limit_bytes=36 * 1024 * 1024
        ),
    )(*in_place)
    context, master, one, two = pl.pallas_call(
        tail_kernel,
        out_shape=(jax.ShapeDtypeStruct(queries.shape, bf16), state, state, state),
        in_specs=[vmem_spec] * 4 + [any_spec] * 3,
        out_specs=(hbm_spec,) * 4,
        scratch_shapes=[pltpu.VMEM(queries.shape, bf16), dma((6 + parts,))],
        compiler_params=pltpu.CompilerParams(vmem_limit_bytes=16 * 1024 * 1024),
    )(query, old, mass, fresh, master, one, two)
    return (master, one, two, context)


beta_one = 0.9
beta_two = 0.95
learning_rate = 0.001
weight_decay = 0.1
epsilon = 1e-08
first_bias = 1.0 - 0.9**10
second_bias = 1.0 - 0.95**10


def adamw_update(gradient, master, moment_one, moment_two):
    new_one = beta_one * moment_one + (1.0 - beta_one) * gradient
    new_two = beta_two * moment_two + (1.0 - beta_two) * gradient * gradient
    update = new_one / first_bias / (jnp.sqrt(new_two / second_bias) + epsilon)
    new_master = master - learning_rate * (update + weight_decay * master)
    return (new_one, new_two, new_master)


def attend(queries, kv_cache, fresh_keys, fresh_values, lengths):
    row_count = queries.shape[0]
    step_count = queries.shape[1]
    kv_heads = fresh_keys.shape[2]
    cache_len = kv_cache.shape[1]
    grouped = queries.reshape(row_count, step_count, kv_heads, -1, HD)
    cached_keys = kv_cache[:, :, 0].reshape(row_count, cache_len, kv_heads, HD)
    cached_values = kv_cache[:, :, 1].reshape(row_count, cache_len, kv_heads, HD)
    scaling = 1.0 / jnp.sqrt(jnp.float32(HD))
    cached_scores = (
        jnp.einsum("rsgqd,rcgd->rsgqc", grouped, cached_keys, preferred_element_type=jnp.float32)
        * scaling
    )
    fresh_scores = (
        jnp.einsum("rsgqd,rugd->rsgqu", grouped, fresh_keys, preferred_element_type=jnp.float32)
        * scaling
    )
    valid_old = jnp.arange(cache_len, dtype=jnp.int32)[None, :] < lengths[:, None]
    valid_old = valid_old[:, None, None, None, :]
    steps_index = jnp.arange(step_count, dtype=jnp.int32)
    valid_new = (steps_index[None, :] <= steps_index[:, None])[None, :, None, None, :]
    scores = jnp.concatenate(
        [
            jnp.where(valid_old, cached_scores, -jnp.inf),
            jnp.where(valid_new, fresh_scores, -jnp.inf),
        ],
        axis=-1,
    )
    row_max = jnp.max(scores, axis=-1, keepdims=True)
    exponent = jnp.exp(scores - row_max)
    weights = (exponent / jnp.sum(exponent, axis=-1, keepdims=True)).astype(jnp.bfloat16)
    output = jnp.einsum(
        "rsgqc,rcgd->rsgqd",
        weights[..., :cache_len],
        cached_values,
        preferred_element_type=jnp.float32,
    )
    output = output + jnp.einsum(
        "rsgqu,rugd->rsgqd",
        weights[..., cache_len:],
        fresh_values,
        preferred_element_type=jnp.float32,
    )
    return output.astype(jnp.bfloat16).reshape(row_count, step_count, -1)


def on_device(
    grad_parts, master_weight, moment_one, moment_two, layer_inputs, queries, kv_cache, lengths
):
    gradient = lax.psum_scatter(
        grad_parts[0].astype(jnp.float32).astype(jnp.bfloat16),
        "fsdp",
        scatter_dimension=1,
        tiled=True,
    ).astype(jnp.float32)
    new_one, new_two, new_master = adamw_update(gradient, master_weight, moment_one, moment_two)
    rollout_weight = new_master.astype(jnp.bfloat16)
    row_count = layer_inputs.shape[0]
    step_count = layer_inputs.shape[1]
    gathered = lax.all_gather(layer_inputs, "tp", axis=2, tiled=True)
    flattened = gathered.reshape(row_count * step_count, gathered.shape[2])
    projected = jnp.einsum(
        "td,kdc->ktc",
        flattened,
        lax.all_gather(rollout_weight, ("rep", "fsdp"), axis=1, tiled=True),
        preferred_element_type=jnp.float32,
    )
    fresh_pair = projected.astype(jnp.bfloat16).reshape(2, row_count, step_count, -1, HD)
    context = attend(queries, kv_cache, fresh_pair[0], fresh_pair[1], lengths)
    return (new_master, new_one, new_two, context)


def solution(mesh):
    shape = mesh.shape
    fits = shape["rep"] == 4 and shape["tp"] == 4 and shape["fsdp"] == 2
    run = functools.partial(fused_device, shape["rep"]) if fits else on_device
    return jax.shard_map(
        run,
        mesh=mesh,
        in_specs=(
            P("fsdp", None, "rep", "tp"),
            P(None, ("rep", "fsdp"), "tp"),
            P(None, ("rep", "fsdp"), "tp"),
            P(None, ("rep", "fsdp"), "tp"),
            P(("rep", "fsdp"), None, "tp"),
            P(("rep", "fsdp"), None, "tp"),
            P(("rep", "fsdp"), None, None, "tp"),
            P(("rep", "fsdp")),
        ),
        out_specs=(
            P(None, ("rep", "fsdp"), "tp"),
            P(None, ("rep", "fsdp"), "tp"),
            P(None, ("rep", "fsdp"), "tp"),
            P(("rep", "fsdp"), None, "tp"),
        ),
        check_vma=False,
    )
```

```python
import functools

import jax
import jax.numpy as jnp
from jax import lax
from jax.experimental import pallas as pl
from jax.experimental.pallas import tpu as pltpu
from jax.sharding import PartitionSpec as P

HD = 128
MESH = pl.DeviceIdType.MESH
W_CHUNKS = 4
W_EARLY = 2
W_AHEAD = 2
GROUPS = 2
ADAM_SUB = 32
TAIL_ROWS = 8
LOG2E = 1.4426950408889634
LOW = -0.7 * 3.4028234663852886e38


def learner_kernel(
    lengths_hbm, grad_hbm, master_hbm, one_hbm, two_hbm, x_hbm, kv_hbm, q_hbm,
    fresh_out, query_out, old_out, mass_out, master_out, one_out, two_out,
    own_grad, peer_grad, master, one, two, wpair, wbuf, xbuf, xstage, xflat,
    far, far_peer, far_out, far_in, near, near_peer, kv_raw, q_raw, lengths,
    state_sem, local_sem, out_sem, grad_send, grad_recv, x_send, x_recv, stage_recv,
    pair_send, pair_recv, w_send, w_near, w_diag, far_send, far_recv, back_send, back_recv, near_send, near_recv, hello,
):
    r, f, t = lax.axis_index("rep"), lax.axis_index("fsdp"), lax.axis_index("tp")
    nf = 1 - f
    rx = r + 1 - 2 * lax.rem(r, 2)
    ry = lax.rem(r + 2, 4)
    rd = lax.rem(rx + 2, 4)
    partner, dev_x, dev_y = (r, nf, t), (rx, f, t), (ry, f, t)
    pair = t + 1 - 2 * lax.rem(t, 2)
    mirror = 3 - t
    pair_mirror = 3 - pair
    middle = (t == 1) | (t == 2)
    mine = lax.rem((t + 1) // 2, 2)
    theirs = 1 - mine
    depth = master.shape[1]
    half = depth // 2
    chunk = half // W_CHUNKS
    x_rows, x_steps = xbuf.shape[2:4]
    group_rows = x_rows // GROUPS
    group_tokens = group_rows * x_steps
    blocks = wbuf.shape[2] // half

    def state_rows(sub, c):
        return pl.ds(pl.multiple_of(sub * half + c * chunk, chunk), chunk)

    def owner_rows(owner, c):
        return pl.ds(pl.multiple_of(owner * half + c * chunk, chunk), chunk)

    order = []
    for c in range(W_CHUNKS):
        order += [(mine, c), (theirs, c)]

    def features(h, sub):
        return pl.ds(pl.multiple_of(h * depth + sub * half, half), half)

    def some_rows(g):
        return pl.ds(g * group_rows, group_rows)

    def tokens(g):
        return pl.ds(g * group_tokens, group_tokens)

    state_local = []
    for i, sub in enumerate((mine, theirs)):
        at = pl.ds(pl.multiple_of(sub * half, half), half)
        source = pl.ds(pl.multiple_of(f * depth + sub * half, half), half)
        state_local.append([
            pltpu.make_async_copy(hbm, vmem, state_sem.at[j, i])
            for j, (hbm, vmem) in enumerate((
                (grad_hbm.at[0, :, source, :], own_grad.at[:, at, :]),
                (master_hbm.at[:, at, :], master.at[:, at, :]),
                (one_hbm.at[:, at, :], one.at[:, at, :]),
                (two_hbm.at[:, at, :], two.at[:, at, :]),
            ))
        ])
        for copy in state_local[i]:
            copy.start()
    local = [
        pltpu.make_async_copy(x_hbm.at[:, :, features(f, mine)], xbuf.at[t, f], local_sem.at[0]),
        pltpu.make_async_copy(kv_hbm, kv_raw, local_sem.at[1]),
        pltpu.make_async_copy(q_hbm, q_raw, local_sem.at[2]),
        pltpu.make_async_copy(lengths_hbm, lengths, local_sem.at[3]),
    ]
    barrier = pltpu.get_barrier_semaphore()

    def greet(device):
        pl.semaphore_signal(barrier, inc=1, device_id=device, device_id_type=MESH)

    for device in (partner, dev_x, dev_y, (r, 0, pair), (r, 1, pair)):
        greet(device)

    @pl.when(middle)
    def _():
        for h in range(2):
            greet((r, h, mirror))

    pl.semaphore_wait(barrier, jnp.where(middle, 7, 5))

    @pl.when(middle)
    def _():
        pl.semaphore_signal(hello.at[0], inc=1, device_id=(r, f, mirror), device_id_type=MESH)

    def remote(src, dst, send, recv, device):
        return pltpu.make_async_remote_copy(
            src_ref=src, dst_ref=dst, send_sem=send, recv_sem=recv,
            device_id=device, device_id_type=MESH,
        )

    def drain(ref, sem):
        remote(ref, ref, sem, sem, partner).wait_send()

    def landed(ref, sem):
        remote(ref, ref, sem, sem, partner).wait_recv()

    def grad_copy(i):
        sub, c = order[i]
        source = pl.ds(pl.multiple_of(nf * depth + sub * half + c * chunk, chunk), chunk)
        return remote(
            grad_hbm.at[0, :, source, :], peer_grad.at[:, state_rows(sub, c), :],
            grad_send.at[0], grad_recv.at[i], partner,
        )

    def x_own(g, h, sub, slot, device):
        remote(
            x_hbm.at[some_rows(g), :, features(h, sub)], xbuf.at[t, f, some_rows(g)],
            x_send.at[slot], x_recv.at[t, g], device,
        ).start()

    def x_swap(g):
        x_own(g, nf, mine, 0, partner)

    def x_mirror(g):
        for h in range(2):
            x_own(g, h, mine, 1, (r, h, mirror))

    def x_pair(g, h):
        x_own(g, h, theirs, 2, (r, h, pair))

    def x_pair_mirror(g):
        for h in range(2):
            x_own(g, h, theirs, 3, (r, h, pair_mirror))

    def x_arrived(k, g):
        landed(xbuf.at[k, :, some_rows(g)], x_recv.at[k, g])

    def relay(g):
        x_arrived(pair, g)
        remote(
            xbuf.at[pair, :, some_rows(g)], xbuf.at[pair, :, some_rows(g)],
            x_send.at[4], x_recv.at[pair, g], (r, f, mirror),
        ).start()

    def x_stage(h):
        remote(
            x_hbm.at[some_rows(0), :, features(h, theirs)], xstage.at[f],
            x_send.at[3], stage_recv.at[0], (r, h, mirror),
        ).start()

    def unstage():
        landed(xstage, stage_recv.at[0])
        remote(
            xstage, xbuf.at[mirror, :, some_rows(0)], x_send.at[5], x_recv.at[mirror, 0], (r, f, pair)
        ).start()

    def w_pair(c):
        return remote(
            wpair.at[:, pl.ds(c * chunk, chunk), :], wbuf.at[1, :, owner_rows(r, c), :],
            pair_send.at[0], pair_recv.at[c], (r, f, pair),
        )

    def w_go(cg, c):
        at = wbuf.at[cg, :, owner_rows(r, c), :]
        remote(at, at, w_send.at[0], w_near.at[cg, c], dev_x).start()
        remote(at, at, w_send.at[1], w_near.at[cg, c], dev_y).start()

    def w_step(cg, c):
        landed(wbuf.at[cg, :, pl.ds(0, 2 * chunk), :], w_near.at[cg, c])
        for kv, owner, device in ((0, rx, dev_y), (1, ry, dev_x)):
            at = wbuf.at[cg, kv, owner_rows(owner, c), :]
            remote(at, at, w_send.at[2], w_diag.at[cg, c], device).start()

    def w_last(cg, c):
        landed(wbuf.at[cg, :, owner_rows(rd, c), :], w_diag.at[cg, c])

    def pair_step(c):
        w_pair(c).wait_recv()
        w_go(1, c)

    grad_copy(0).start()

    @pl.when(middle)
    def _():
        x_pair(0, 0)
        x_mirror(0)
        x_mirror(1)
        x_stage(0)
        x_stage(1)

    @pl.when(jnp.logical_not(middle))
    def _():
        x_pair(0, 0)
        x_pair(0, 1)

    for i in range(1, len(order)):
        grad_copy(i).start()

    first_bias = 1.0 - 0.9**10
    second_bias = 1.0 - 0.95**10

    def adam(sub, c, out, base):
        def piece(i, carry):
            at = pl.ds(pl.multiple_of(sub * half + c * chunk + i * ADAM_SUB, ADAM_SUB), ADAM_SUB)
            gradient = own_grad[:, at, :].astype(jnp.float32) + peer_grad[:, at, :].astype(jnp.float32)
            new_one = 0.9 * one[:, at, :] + (1.0 - 0.9) * gradient
            new_two = 0.95 * two[:, at, :] + (1.0 - 0.95) * gradient * gradient
            update = new_one / first_bias / (jnp.sqrt(new_two / second_bias) + 1e-08)
            old = master[:, at, :]
            new_master = old - 0.001 * (update + 0.1 * old)
            one[:, at, :] = new_one
            two[:, at, :] = new_two
            master[:, at, :] = new_master
            to = pl.ds(pl.multiple_of(base + c * chunk + i * ADAM_SUB, ADAM_SUB), ADAM_SUB)
            out[:, to, :] = new_master.astype(jnp.bfloat16)
            return carry

        lax.fori_loop(0, chunk // ADAM_SUB, piece, 0)

    for i, (sub, c) in enumerate(order):
        if i < 2:
            for copy in state_local[i]:
                copy.wait()
        grad_copy(i).wait_recv()
        if i % 2 == 1:
            adam(sub, c, wpair, 0)
            w_pair(c).start()
        else:
            adam(sub, c, wbuf.at[0], r * half)
            if c < W_EARLY:
                w_go(0, c)
    outs = [
        pltpu.make_async_copy(master, master_out, out_sem.at[0]),
        pltpu.make_async_copy(one, one_out, out_sem.at[1]),
        pltpu.make_async_copy(two, two_out, out_sem.at[2]),
    ]
    for copy in local:
        copy.start()
    for g in range(GROUPS):
        x_swap(g)

    kv_rows, cache_len = kv_raw.shape[:2]
    parts = kv_rows // TAIL_ROWS
    head = HD
    groups = kv_raw.shape[3] // head
    per_group = q_raw.shape[2] // head // groups
    part_tokens = TAIL_ROWS * x_steps
    keys = TAIL_ROWS * cache_len
    column = lax.broadcasted_iota(jnp.int32, (1, keys), 1)
    key_row = column // cache_len
    position = column - key_row * cache_len
    token_row = lax.broadcasted_iota(jnp.int32, (part_tokens, 1), 0) // x_steps
    factor = head**-0.5 * LOG2E

    def cached_part(part):
        mine_rows = slice(part * TAIL_ROWS, (part + 1) * TAIL_ROWS)
        limit = jnp.zeros((1, keys), jnp.int32)
        for at in range(TAIL_ROWS):
            limit = jnp.where(key_row == at, lengths[part * TAIL_ROWS + at], limit)
        valid = jnp.where(position < limit, key_row, -1) == token_row
        for group in range(groups):
            cols = slice(group * head, (group + 1) * head)
            query = jnp.concatenate(
                [
                    q_raw[mine_rows, :, (group * per_group + h) * head : (group * per_group + h + 1) * head].reshape(
                        part_tokens, head
                    )
                    for h in range(per_group)
                ],
                axis=0,
            )
            key = kv_raw[mine_rows, :, 0, cols].reshape(keys, head)
            value = kv_raw[mine_rows, :, 1, cols].reshape(keys, head)
            scores = lax.dot_general(query, key, (((1,), (1,)), ((), ())), preferred_element_type=jnp.float32)
            scores = jnp.where(valid[None], scores.reshape(per_group, part_tokens, keys), LOW)
            scores = scores.reshape(per_group * part_tokens, keys)
            top = jnp.max(scores, axis=-1, keepdims=True)
            weights = jnp.exp2((scores - top) * factor)
            total = jnp.sum(weights, axis=-1, keepdims=True)
            old = jnp.dot(weights.astype(jnp.bfloat16), value, preferred_element_type=jnp.float32)
            where = part * groups + group
            query_out[where] = query
            old_out[where] = old * (1.0 / total)
            mass_out[where] = jnp.broadcast_to(top + jnp.log2(total) * (1.0 / factor), old.shape)

    @pl.when(middle)
    def _():
        pl.semaphore_wait(hello.at[0], 1)
        pl.semaphore_signal(hello.at[1], inc=1, device_id=(r, f, pair), device_id_type=MESH)
        relay(0)

    @pl.when(jnp.logical_not(middle))
    def _():
        x_pair(1, 0)
        x_pair(1, 1)

    def send_next(item):
        cg, c = item
        if cg == 1:
            pair_step(c)
        else:
            w_go(0, c)

    items = [(0, c) for c in range(W_EARLY)] + [(1, c) for c in range(W_CHUNKS)]
    items += [(0, c) for c in range(W_EARLY, W_CHUNKS)]
    sent = W_EARLY
    for c in range(W_EARLY):
        w_step(0, c)
    for copy in local:
        copy.wait()
    for i in range(W_EARLY + W_CHUNKS):
        if i >= W_EARLY:
            w_step(*items[i])
        while sent < min(i + W_AHEAD + 1, len(items)):
            send_next(items[sent])
            sent += 1
        if i == 1:
            @pl.when(middle)
            def _():
                x_pair(0, 1)
                unstage()

        if i == 2:
            @pl.when(middle)
            def _():
                x_pair(1, 0)
                x_pair(1, 1)
                relay(1)

            @pl.when(jnp.logical_not(middle))
            def _():
                pl.semaphore_wait(hello.at[1], 1)
                x_mirror(0)
                x_mirror(1)

        if i == 3:
            for copy in outs:
                copy.start()

            @pl.when(middle)
            def _():
                x_pair_mirror(1)

        if i < parts:
            cached_part(i)
    for part in range(W_EARLY + W_CHUNKS, parts):
        cached_part(part)

    def far_swap(g):
        return remote(
            far.at[nf, :, tokens(g), :], far_peer.at[:, tokens(g), :], far_send.at[0], far_recv.at[g], partner
        )

    def far_back(g):
        return remote(
            far_out.at[:, tokens(g), :], far_in.at[:, tokens(g), :], back_send.at[0], back_recv.at[g], (r, f, pair)
        )

    def near_swap(g):
        return remote(
            near.at[nf, :, tokens(g), :], near_peer.at[:, tokens(g), :], near_send.at[0], near_recv.at[g], partner
        )

    def flatten(g):
        def one_block(k, carry):
            for th in range(2):
                piece = xbuf[k, th, some_rows(g)].reshape(group_tokens, half)
                xflat[g, pl.ds(th * group_tokens, group_tokens), pl.ds(pl.multiple_of(k * half, half), half)] = piece
            return carry

        lax.fori_loop(0, blocks, one_block, 0)

    def multiply(cg, out, g, start, stop):
        for kv in range(2):
            total = None
            if stop - start == W_CHUNKS:
                total = jnp.dot(xflat[g], wbuf[cg, kv], preferred_element_type=jnp.float32)
            else:
                for k in range(blocks):
                    at = slice(k * half + start * chunk, k * half + stop * chunk)
                    product = jnp.dot(xflat[g, :, at], wbuf[cg, kv, at, :], preferred_element_type=jnp.float32)
                    total = product if total is None else total + product
            for th in range(2):
                piece = total[th * group_tokens : (th + 1) * group_tokens]
                if start > 0:
                    out[th, kv, tokens(g), :] += piece
                else:
                    out[th, kv, tokens(g), :] = piece

    def far_done(g):
        far_swap(g).wait_recv()
        both = far[f, :, tokens(g), :] + far_peer[:, tokens(g), :]
        far_out[:, tokens(g), :] = both.astype(jnp.bfloat16)
        far_back(g).start()

    def x_ready(g):
        landed(xbuf.at[t, nf, some_rows(g)], x_recv.at[t, g])
        x_arrived(mirror, g)
        x_arrived(pair_mirror, g)
        flatten(g)

    for c in range(W_EARLY):
        w_last(0, c)
        w_last(1, c)

    @pl.when(middle)
    def _():
        x_ready(0)
        multiply(1, far, 0, 0, W_EARLY)
        multiply(0, near, 0, 0, W_EARLY)

    for c in range(W_EARLY, W_CHUNKS - 1):
        w_step(0, c)

    @pl.when(jnp.logical_not(middle))
    def _():
        x_arrived(pair, 0)
        x_ready(0)
        multiply(1, far, 0, 0, W_EARLY)
        multiply(0, near, 0, 0, W_EARLY)

    @pl.when(middle)
    def _():
        x_ready(1)
        multiply(1, far, 1, 0, W_EARLY)

    for c in range(W_EARLY, W_CHUNKS):
        w_last(1, c)
    multiply(1, far, 0, W_EARLY, W_CHUNKS)
    far_swap(0).start()

    @pl.when(middle)
    def _():
        multiply(1, far, 1, W_EARLY, W_CHUNKS)
        far_swap(1).start()

    far_done(0)
    w_step(0, W_CHUNKS - 1)

    @pl.when(jnp.logical_not(middle))
    def _():
        x_arrived(pair, 1)
        x_ready(1)
        multiply(1, far, 1, 0, W_CHUNKS)
        far_swap(1).start()

    @pl.when(middle)
    def _():
        far_done(1)

    multiply(0, near, 1, 0, W_EARLY)

    @pl.when(jnp.logical_not(middle))
    def _():
        far_done(1)

    for c in range(W_EARLY, W_CHUNKS):
        w_last(0, c)
    for g in range(GROUPS):
        multiply(0, near, g, W_EARLY, W_CHUNKS)
        near_swap(g).start()

    drain(peer_grad, grad_send.at[0])
    drain(xbuf.at[0, 0], x_send.at[0])
    drain(xbuf.at[0], x_send.at[1])
    drain(xbuf.at[0], x_send.at[2])

    @pl.when(middle)
    def _():
        drain(xbuf.at[0], x_send.at[3])
        drain(xbuf.at[0], x_send.at[4])
        drain(xstage, x_send.at[5])

    drain(wpair, pair_send.at[0])
    for way in range(3):
        drain(wbuf.at[:, :, pl.ds(0, half), :], w_send.at[way])
    drain(far.at[0], far_send.at[0])
    drain(far_out, back_send.at[0])
    for copy in outs:
        copy.wait()
    for g in range(GROUPS):
        near_swap(g).wait_recv()
    for g in range(GROUPS):
        far_back(g).wait_recv()
    fresh_out[...] = (near[f] + near_peer[...] + far_in[...].astype(jnp.float32)).astype(jnp.bfloat16)
    drain(near.at[0], near_send.at[0])


def tail_kernel(
    query_ref, old_ref, mass_ref, fresh_ref, master_in, one_in, two_in,
    context, master_out, one_out, two_out, out_ref, sem,
):
    moves = [
        pltpu.make_async_copy(source.at[kv], target.at[kv], sem.at[2 * i + kv])
        for i, (source, target) in enumerate(((master_in, master_out), (one_in, one_out), (two_in, two_out)))
        for kv in range(2)
    ]
    for move in moves:
        move.start()
    row_count, step_count, features = out_ref.shape
    head = HD
    groups = fresh_ref.shape[2] // head
    per_group = features // head // groups
    tokens = TAIL_ROWS * step_count
    parts = row_count // TAIL_ROWS
    token = lax.broadcasted_iota(jnp.int32, (tokens, 1), 0)
    column = lax.broadcasted_iota(jnp.int32, (1, tokens), 1)
    valid = (column // step_count == token // step_count) & (column <= token)
    factor = head**-0.5 * LOG2E
    contract = (((1,), (1,)), ((), ()))
    writes = []
    for part in range(parts):
        here = slice(part * tokens, (part + 1) * tokens)
        mine = slice(part * TAIL_ROWS, (part + 1) * TAIL_ROWS)
        for group in range(groups):
            cols = slice(group * head, (group + 1) * head)
            where = part * groups + group
            scores = lax.dot_general(
                query_ref[where], fresh_ref[0, here, cols], contract, preferred_element_type=jnp.float32
            )
            scores = jnp.where(valid[None], scores.reshape(per_group, tokens, tokens), LOW)
            scores = scores.reshape(per_group * tokens, tokens)
            mass = mass_ref[where]
            top = jnp.maximum(mass, jnp.max(scores, axis=-1, keepdims=True))
            old_weight = jnp.exp2((mass - top) * factor)
            weights = jnp.exp2((scores - top[:, :tokens]) * factor)
            scale = 1.0 / (old_weight + jnp.sum(weights, axis=-1, keepdims=True))
            new = jnp.dot(weights.astype(jnp.bfloat16), fresh_ref[1, here, cols], preferred_element_type=jnp.float32)
            out = (old_weight * old_ref[where] + new) * scale
            for h in range(per_group):
                at = (group * per_group + h) * head
                piece = out[h * tokens : (h + 1) * tokens].reshape(TAIL_ROWS, step_count, head)
                out_ref[mine, :, at : at + head] = piece.astype(jnp.bfloat16)
        write = pltpu.make_async_copy(out_ref.at[mine], context.at[mine], sem.at[6 + part])
        write.start()
        writes.append(write)
    for write in writes + moves:
        write.wait()


def fused_device(n_rep, grad_parts, master_weight, moment_one, moment_two, layer_inputs, queries, kv_cache, lengths):
    row_count, step_count, features = layer_inputs.shape
    _, depth, width = master_weight.shape
    n_tp = n_rep
    tokens = row_count * step_count
    bf16, f32 = jnp.bfloat16, jnp.float32
    dma = pltpu.SemaphoreType.DMA
    state = jax.ShapeDtypeStruct(master_weight.shape, f32)
    any_spec = pl.BlockSpec(memory_space=pl.ANY)
    hbm_spec = pl.BlockSpec(memory_space=pltpu.HBM)
    in_place = [
        pltpu.with_memory_space_constraint(array, pltpu.HBM)
        for array in (lengths, grad_parts, master_weight, moment_one, moment_two, layer_inputs, kv_cache, queries)
    ]
    half = depth // 2
    vmem_spec = pl.BlockSpec(memory_space=pltpu.VMEM)
    parts = row_count // TAIL_ROWS
    groups = width // HD
    stacked = (parts * groups, queries.shape[2] // width * TAIL_ROWS * step_count, HD)
    fresh, query, old, mass, master, one, two = pl.pallas_call(
        learner_kernel,
        out_shape=(
            jax.ShapeDtypeStruct((2, tokens, width), bf16),
            jax.ShapeDtypeStruct(stacked, bf16),
            jax.ShapeDtypeStruct(stacked, f32),
            jax.ShapeDtypeStruct(stacked, f32),
            state,
            state,
            state,
        ),
        in_specs=[hbm_spec] * 8,
        out_specs=(vmem_spec,) * 4 + (any_spec,) * 3,
        scratch_shapes=[
            pltpu.VMEM((2, depth, width), bf16),
            pltpu.VMEM((2, depth, width), bf16),
            pltpu.VMEM((2, depth, width), f32),
            pltpu.VMEM((2, depth, width), f32),
            pltpu.VMEM((2, depth, width), f32),
            pltpu.VMEM((2, half, width), bf16),
            pltpu.VMEM((2, 2, n_rep * half, width), bf16),
            pltpu.VMEM((n_tp, 2, row_count, step_count, half), bf16),
            pltpu.VMEM((2, row_count // GROUPS, step_count, half), bf16),
            pltpu.VMEM((GROUPS, 2 * tokens // GROUPS, n_tp * half), bf16),
            pltpu.VMEM((2, 2, tokens, width), f32),
            pltpu.VMEM((2, tokens, width), f32),
            pltpu.VMEM((2, tokens, width), bf16),
            pltpu.VMEM((2, tokens, width), bf16),
            pltpu.VMEM((2, 2, tokens, width), f32),
            pltpu.VMEM((2, tokens, width), f32),
            pltpu.VMEM(kv_cache.shape, bf16),
            pltpu.VMEM(queries.shape, bf16),
            pltpu.SMEM(lengths.shape, jnp.int32),
            dma((4, 2)),
            dma((4,)),
            dma((3,)),
            dma((1,)),
            dma((2 * W_CHUNKS,)),
            dma((6,)),
            dma((n_tp, GROUPS)),
            dma((1,)),
            dma((1,)),
            dma((W_CHUNKS,)),
            dma((3,)),
            dma((2, W_CHUNKS)),
            dma((2, W_CHUNKS)),
            dma((1,)),
            dma((GROUPS,)),
            dma((1,)),
            dma((GROUPS,)),
            dma((1,)),
            dma((GROUPS,)),
            pltpu.SemaphoreType.REGULAR((2,)),
        ],
        compiler_params=pltpu.CompilerParams(
            collective_id=0, has_side_effects=True, vmem_limit_bytes=36 * 1024 * 1024
        ),
    )(*in_place)
    context, master, one, two = pl.pallas_call(
        tail_kernel,
        out_shape=(jax.ShapeDtypeStruct(queries.shape, bf16), state, state, state),
        in_specs=[vmem_spec] * 4 + [any_spec] * 3,
        out_specs=(hbm_spec,) * 4,
        scratch_shapes=[pltpu.VMEM(queries.shape, bf16), dma((6 + parts,))],
        compiler_params=pltpu.CompilerParams(vmem_limit_bytes=16 * 1024 * 1024),
    )(query, old, mass, fresh, master, one, two)
    return (master, one, two, context)


beta_one = 0.9
beta_two = 0.95
learning_rate = 0.001
weight_decay = 0.1
epsilon = 1e-08
first_bias = 1.0 - 0.9**10
second_bias = 1.0 - 0.95**10


def adamw_update(gradient, master, moment_one, moment_two):
    new_one = beta_one * moment_one + (1.0 - beta_one) * gradient
    new_two = beta_two * moment_two + (1.0 - beta_two) * gradient * gradient
    update = new_one / first_bias / (jnp.sqrt(new_two / second_bias) + epsilon)
    new_master = master - learning_rate * (update + weight_decay * master)
    return (new_one, new_two, new_master)


def attend(queries, kv_cache, fresh_keys, fresh_values, lengths):
    row_count = queries.shape[0]
    step_count = queries.shape[1]
    kv_heads = fresh_keys.shape[2]
    cache_len = kv_cache.shape[1]
    grouped = queries.reshape(row_count, step_count, kv_heads, -1, HD)
    cached_keys = kv_cache[:, :, 0].reshape(row_count, cache_len, kv_heads, HD)
    cached_values = kv_cache[:, :, 1].reshape(row_count, cache_len, kv_heads, HD)
    scaling = 1.0 / jnp.sqrt(jnp.float32(HD))
    cached_scores = (
        jnp.einsum("rsgqd,rcgd->rsgqc", grouped, cached_keys, preferred_element_type=jnp.float32)
        * scaling
    )
    fresh_scores = (
        jnp.einsum("rsgqd,rugd->rsgqu", grouped, fresh_keys, preferred_element_type=jnp.float32)
        * scaling
    )
    valid_old = jnp.arange(cache_len, dtype=jnp.int32)[None, :] < lengths[:, None]
    valid_old = valid_old[:, None, None, None, :]
    steps_index = jnp.arange(step_count, dtype=jnp.int32)
    valid_new = (steps_index[None, :] <= steps_index[:, None])[None, :, None, None, :]
    scores = jnp.concatenate(
        [
            jnp.where(valid_old, cached_scores, -jnp.inf),
            jnp.where(valid_new, fresh_scores, -jnp.inf),
        ],
        axis=-1,
    )
    row_max = jnp.max(scores, axis=-1, keepdims=True)
    exponent = jnp.exp(scores - row_max)
    weights = (exponent / jnp.sum(exponent, axis=-1, keepdims=True)).astype(jnp.bfloat16)
    output = jnp.einsum(
        "rsgqc,rcgd->rsgqd",
        weights[..., :cache_len],
        cached_values,
        preferred_element_type=jnp.float32,
    )
    output = output + jnp.einsum(
        "rsgqu,rugd->rsgqd",
        weights[..., cache_len:],
        fresh_values,
        preferred_element_type=jnp.float32,
    )
    return output.astype(jnp.bfloat16).reshape(row_count, step_count, -1)


def on_device(
    grad_parts, master_weight, moment_one, moment_two, layer_inputs, queries, kv_cache, lengths
):
    gradient = lax.psum_scatter(
        grad_parts[0].astype(jnp.float32).astype(jnp.bfloat16),
        "fsdp",
        scatter_dimension=1,
        tiled=True,
    ).astype(jnp.float32)
    new_one, new_two, new_master = adamw_update(gradient, master_weight, moment_one, moment_two)
    rollout_weight = new_master.astype(jnp.bfloat16)
    row_count = layer_inputs.shape[0]
    step_count = layer_inputs.shape[1]
    gathered = lax.all_gather(layer_inputs, "tp", axis=2, tiled=True)
    flattened = gathered.reshape(row_count * step_count, gathered.shape[2])
    projected = jnp.einsum(
        "td,kdc->ktc",
        flattened,
        lax.all_gather(rollout_weight, ("rep", "fsdp"), axis=1, tiled=True),
        preferred_element_type=jnp.float32,
    )
    fresh_pair = projected.astype(jnp.bfloat16).reshape(2, row_count, step_count, -1, HD)
    context = attend(queries, kv_cache, fresh_pair[0], fresh_pair[1], lengths)
    return (new_master, new_one, new_two, context)


def solution(mesh):
    shape = mesh.shape
    fits = shape["rep"] == 4 and shape["tp"] == 4 and shape["fsdp"] == 2
    run = functools.partial(fused_device, shape["rep"]) if fits else on_device
    return jax.shard_map(
        run,
        mesh=mesh,
        in_specs=(
            P("fsdp", None, "rep", "tp"),
            P(None, ("rep", "fsdp"), "tp"),
            P(None, ("rep", "fsdp"), "tp"),
            P(None, ("rep", "fsdp"), "tp"),
            P(("rep", "fsdp"), None, "tp"),
            P(("rep", "fsdp"), None, "tp"),
            P(("rep", "fsdp"), None, None, "tp"),
            P(("rep", "fsdp")),
        ),
        out_specs=(
            P(None, ("rep", "fsdp"), "tp"),
            P(None, ("rep", "fsdp"), "tp"),
            P(None, ("rep", "fsdp"), "tp"),
            P(("rep", "fsdp"), None, "tp"),
        ),
        check_vma=False,
    )
```

```python
import functools

import jax
import jax.numpy as jnp
from jax import lax
from jax.experimental import pallas as pl
from jax.experimental.pallas import tpu as pltpu
from jax.sharding import PartitionSpec as P

HD = 128
MESH = pl.DeviceIdType.MESH
W_CHUNKS = 4
W_EARLY = 2
W_AHEAD = 2
GROUPS = 2
ADAM_SUB = 32
TAIL_ROWS = 8
LOG2E = 1.4426950408889634
LOW = -0.7 * 3.4028234663852886e38


def learner_kernel(
    lengths_hbm, grad_hbm, master_hbm, one_hbm, two_hbm, x_hbm, kv_hbm, q_hbm,
    fresh_out, query_out, old_out, mass_out, master_out, one_out, two_out,
    own_grad, peer_grad, master, one, two, wpair, wbuf, xbuf, xstage, xflat,
    far, far_peer, far_out, far_in, near, near_peer, kv_raw, q_raw, lengths,
    state_sem, local_sem, out_sem, grad_send, grad_recv, x_send, x_recv, stage_recv,
    pair_send, pair_recv, w_send, w_near, w_diag, far_send, far_recv, back_send, back_recv, near_send, near_recv, hello,
):
    r, f, t = lax.axis_index("rep"), lax.axis_index("fsdp"), lax.axis_index("tp")
    nf = 1 - f
    rx = r + 1 - 2 * lax.rem(r, 2)
    ry = lax.rem(r + 2, 4)
    rd = lax.rem(rx + 2, 4)
    partner, dev_x, dev_y = (r, nf, t), (rx, f, t), (ry, f, t)
    pair = t + 1 - 2 * lax.rem(t, 2)
    mirror = 3 - t
    pair_mirror = 3 - pair
    middle = (t == 1) | (t == 2)
    mine = lax.rem((t + 1) // 2, 2)
    theirs = 1 - mine
    depth = master.shape[1]
    half = depth // 2
    chunk = half // W_CHUNKS
    x_rows, x_steps = xbuf.shape[2:4]
    group_rows = x_rows // GROUPS
    group_tokens = group_rows * x_steps
    blocks = wbuf.shape[2] // half

    def state_rows(sub, c):
        return pl.ds(pl.multiple_of(sub * half + c * chunk, chunk), chunk)

    def owner_rows(owner, c):
        return pl.ds(pl.multiple_of(owner * half + c * chunk, chunk), chunk)

    order = []
    for c in range(W_CHUNKS):
        order += [(mine, c), (theirs, c)]

    def features(h, sub):
        return pl.ds(pl.multiple_of(h * depth + sub * half, half), half)

    def some_rows(g):
        return pl.ds(g * group_rows, group_rows)

    def tokens(g):
        return pl.ds(g * group_tokens, group_tokens)

    barrier = pltpu.get_barrier_semaphore()

    def greet(device):
        pl.semaphore_signal(barrier, inc=1, device_id=device, device_id_type=MESH)

    for device in (partner, dev_x, dev_y, (r, 0, pair), (r, 1, pair)):
        greet(device)

    @pl.when(middle)
    def _():
        for h in range(2):
            greet((r, h, mirror))

    state_local = []
    for i, sub in enumerate((mine, theirs)):
        at = pl.ds(pl.multiple_of(sub * half, half), half)
        source = pl.ds(pl.multiple_of(f * depth + sub * half, half), half)
        state_local.append([
            pltpu.make_async_copy(hbm, vmem, state_sem.at[j, i])
            for j, (hbm, vmem) in enumerate((
                (grad_hbm.at[0, :, source, :], own_grad.at[:, at, :]),
                (master_hbm.at[:, at, :], master.at[:, at, :]),
                (one_hbm.at[:, at, :], one.at[:, at, :]),
                (two_hbm.at[:, at, :], two.at[:, at, :]),
            ))
        ])
        for copy in state_local[i]:
            copy.start()
    local = [
        pltpu.make_async_copy(x_hbm.at[:, :, features(f, mine)], xbuf.at[t, f], local_sem.at[0]),
        pltpu.make_async_copy(kv_hbm, kv_raw, local_sem.at[1]),
        pltpu.make_async_copy(q_hbm, q_raw, local_sem.at[2]),
        pltpu.make_async_copy(lengths_hbm, lengths, local_sem.at[3]),
    ]
    pl.semaphore_wait(barrier, jnp.where(middle, 7, 5))

    @pl.when(middle)
    def _():
        pl.semaphore_signal(hello.at[0], inc=1, device_id=(r, f, mirror), device_id_type=MESH)

    def remote(src, dst, send, recv, device):
        return pltpu.make_async_remote_copy(
            src_ref=src, dst_ref=dst, send_sem=send, recv_sem=recv,
            device_id=device, device_id_type=MESH,
        )

    def drain(ref, sem):
        remote(ref, ref, sem, sem, partner).wait_send()

    def landed(ref, sem):
        remote(ref, ref, sem, sem, partner).wait_recv()

    def grad_copy(i):
        sub, c = order[i]
        source = pl.ds(pl.multiple_of(nf * depth + sub * half + c * chunk, chunk), chunk)
        return remote(
            grad_hbm.at[0, :, source, :], peer_grad.at[:, state_rows(sub, c), :],
            grad_send.at[0], grad_recv.at[i], partner,
        )

    def x_own(g, h, sub, slot, device):
        remote(
            x_hbm.at[some_rows(g), :, features(h, sub)], xbuf.at[t, f, some_rows(g)],
            x_send.at[slot], x_recv.at[t, g], device,
        ).start()

    def x_swap(g):
        x_own(g, nf, mine, 0, partner)

    def x_mirror(g):
        for h in range(2):
            x_own(g, h, mine, 1, (r, h, mirror))

    def x_pair(g, h):
        x_own(g, h, theirs, 1, (r, h, pair))

    def x_pair_mirror(g):
        for h in range(2):
            x_own(g, h, theirs, 2, (r, h, pair_mirror))

    def x_arrived(k, g):
        landed(xbuf.at[k, :, some_rows(g)], x_recv.at[k, g])

    def relay(g):
        x_arrived(pair, g)
        remote(
            xbuf.at[pair, :, some_rows(g)], xbuf.at[pair, :, some_rows(g)],
            x_send.at[2], x_recv.at[pair, g], (r, f, mirror),
        ).start()

    def x_stage(h):
        remote(
            x_hbm.at[some_rows(0), :, features(h, theirs)], xstage.at[f],
            x_send.at[2], stage_recv.at[0], (r, h, mirror),
        ).start()

    def unstage():
        landed(xstage, stage_recv.at[0])
        remote(
            xstage, xbuf.at[mirror, :, some_rows(0)], x_send.at[3], x_recv.at[mirror, 0], (r, f, pair)
        ).start()

    def w_pair(c):
        return remote(
            wpair.at[:, pl.ds(c * chunk, chunk), :], wbuf.at[1, :, owner_rows(r, c), :],
            pair_send.at[0], pair_recv.at[c], (r, f, pair),
        )

    def w_go(cg, c):
        at = wbuf.at[cg, :, owner_rows(r, c), :]
        remote(at, at, w_send.at[0], w_near.at[cg, c], dev_x).start()
        remote(at, at, w_send.at[0], w_near.at[cg, c], dev_y).start()

    def w_step(cg, c):
        landed(wbuf.at[cg, :, pl.ds(0, 2 * chunk), :], w_near.at[cg, c])
        for kv, owner, device in ((0, rx, dev_y), (1, ry, dev_x)):
            at = wbuf.at[cg, kv, owner_rows(owner, c), :]
            remote(at, at, w_send.at[0], w_diag.at[cg, c // W_EARLY], device).start()

    def w_last(cg, late):
        landed(wbuf.at[cg, :, pl.ds(0, W_EARLY * chunk), :], w_diag.at[cg, late])

    def pair_step(c):
        w_pair(c).wait_recv()
        w_go(1, c)

    grad_copy(0).start()

    @pl.when(middle)
    def _():
        x_pair(0, 0)
        x_stage(0)
        x_stage(1)
        x_mirror(0)
        x_mirror(1)

    @pl.when(jnp.logical_not(middle))
    def _():
        x_pair(0, 0)
        x_pair(0, 1)

    for i in range(1, len(order)):
        grad_copy(i).start()

    first_bias = 1.0 - 0.9**10
    second_bias = 1.0 - 0.95**10

    def adam(sub, c, out, base):
        def piece(i, carry):
            at = pl.ds(pl.multiple_of(sub * half + c * chunk + i * ADAM_SUB, ADAM_SUB), ADAM_SUB)
            gradient = own_grad[:, at, :].astype(jnp.float32) + peer_grad[:, at, :].astype(jnp.float32)
            new_one = 0.9 * one[:, at, :] + (1.0 - 0.9) * gradient
            new_two = 0.95 * two[:, at, :] + (1.0 - 0.95) * gradient * gradient
            update = new_one / first_bias / (jnp.sqrt(new_two / second_bias) + 1e-08)
            old = master[:, at, :]
            new_master = old - 0.001 * (update + 0.1 * old)
            one[:, at, :] = new_one
            two[:, at, :] = new_two
            master[:, at, :] = new_master
            to = pl.ds(pl.multiple_of(base + c * chunk + i * ADAM_SUB, ADAM_SUB), ADAM_SUB)
            out[:, to, :] = new_master.astype(jnp.bfloat16)
            return carry

        lax.fori_loop(0, chunk // ADAM_SUB, piece, 0)

    for i, (sub, c) in enumerate(order):
        if i < 2:
            for copy in state_local[i]:
                copy.wait()
        grad_copy(i).wait_recv()
        if i % 2 == 1:
            adam(sub, c, wpair, 0)
            w_pair(c).start()
        else:
            adam(sub, c, wbuf.at[0], r * half)
            if c < W_EARLY:
                w_go(0, c)
    outs = [
        pltpu.make_async_copy(master, master_out, out_sem.at[0]),
        pltpu.make_async_copy(one, one_out, out_sem.at[1]),
        pltpu.make_async_copy(two, two_out, out_sem.at[2]),
    ]
    for copy in local:
        copy.start()
    for g in range(GROUPS):
        x_swap(g)

    kv_rows, cache_len = kv_raw.shape[:2]
    parts = kv_rows // TAIL_ROWS
    head = HD
    groups = kv_raw.shape[3] // head
    per_group = q_raw.shape[2] // head // groups
    part_tokens = TAIL_ROWS * x_steps
    keys = TAIL_ROWS * cache_len
    column = lax.broadcasted_iota(jnp.int32, (1, keys), 1)
    key_row = column // cache_len
    position = column - key_row * cache_len
    token_row = lax.broadcasted_iota(jnp.int32, (part_tokens, 1), 0) // x_steps
    factor = head**-0.5 * LOG2E

    def cached_part(part):
        mine_rows = slice(part * TAIL_ROWS, (part + 1) * TAIL_ROWS)
        limit = jnp.zeros((1, keys), jnp.int32)
        for at in range(TAIL_ROWS):
            limit = jnp.where(key_row == at, lengths[part * TAIL_ROWS + at], limit)
        valid = jnp.where(position < limit, key_row, -1) == token_row
        for group in range(groups):
            cols = slice(group * head, (group + 1) * head)
            query = jnp.concatenate(
                [
                    q_raw[mine_rows, :, (group * per_group + h) * head : (group * per_group + h + 1) * head].reshape(
                        part_tokens, head
                    )
                    for h in range(per_group)
                ],
                axis=0,
            )
            key = kv_raw[mine_rows, :, 0, cols].reshape(keys, head)
            value = kv_raw[mine_rows, :, 1, cols].reshape(keys, head)
            scores = lax.dot_general(query, key, (((1,), (1,)), ((), ())), preferred_element_type=jnp.float32)
            scores = jnp.where(valid[None], scores.reshape(per_group, part_tokens, keys), LOW)
            scores = scores.reshape(per_group * part_tokens, keys)
            top = jnp.max(scores, axis=-1, keepdims=True)
            weights = jnp.exp2((scores - top) * factor)
            total = jnp.sum(weights, axis=-1, keepdims=True)
            old = jnp.dot(weights.astype(jnp.bfloat16), value, preferred_element_type=jnp.float32)
            where = part * groups + group
            query_out[where] = query
            old_out[where] = old * (1.0 / total)
            mass_out[where] = jnp.broadcast_to(top + jnp.log2(total) * (1.0 / factor), old.shape)

    @pl.when(middle)
    def _():
        pl.semaphore_wait(hello.at[0], 1)
        pl.semaphore_signal(hello.at[1], inc=1, device_id=(r, f, pair), device_id_type=MESH)
        relay(0)

    @pl.when(jnp.logical_not(middle))
    def _():
        x_pair(1, 0)
        x_pair(1, 1)

    def send_next(item):
        cg, c = item
        if cg == 1:
            pair_step(c)
        else:
            w_go(0, c)

    items = [(0, c) for c in range(W_EARLY)] + [(1, c) for c in range(W_CHUNKS)]
    items += [(0, c) for c in range(W_EARLY, W_CHUNKS)]
    sent = W_EARLY
    for c in range(W_EARLY):
        w_step(0, c)
    for copy in local:
        copy.wait()
    for i in range(W_EARLY + W_CHUNKS):
        if i >= W_EARLY:
            w_step(*items[i])
        while sent < min(i + W_AHEAD + 1, len(items)):
            send_next(items[sent])
            sent += 1
        if i == 1:
            @pl.when(middle)
            def _():
                x_pair(0, 1)
                unstage()

        if i == 2:
            @pl.when(middle)
            def _():
                x_pair(1, 0)
                x_pair(1, 1)
                relay(1)

            @pl.when(jnp.logical_not(middle))
            def _():
                pl.semaphore_wait(hello.at[1], 1)
                x_mirror(0)

        if i == 3:
            for copy in outs:
                copy.start()

        if i == 4:
            @pl.when(middle)
            def _():
                x_pair_mirror(1)

            @pl.when(jnp.logical_not(middle))
            def _():
                x_mirror(1)

        if i < parts:
            cached_part(i)
    for part in range(W_EARLY + W_CHUNKS, parts):
        cached_part(part)

    def far_swap(g):
        return remote(
            far.at[nf, :, tokens(g), :], far_peer.at[:, tokens(g), :], far_send.at[0], far_recv.at[g], partner
        )

    def far_back(g):
        return remote(
            far_out.at[:, tokens(g), :], far_in.at[:, tokens(g), :], back_send.at[0], back_recv.at[g], (r, f, pair)
        )

    def near_swap(g):
        return remote(
            near.at[nf, :, tokens(g), :], near_peer.at[:, tokens(g), :], near_send.at[0], near_recv.at[g], partner
        )

    def flatten(g):
        def one_block(k, carry):
            for th in range(2):
                piece = xbuf[k, th, some_rows(g)].reshape(group_tokens, half)
                xflat[g, pl.ds(th * group_tokens, group_tokens), pl.ds(pl.multiple_of(k * half, half), half)] = piece
            return carry

        lax.fori_loop(0, blocks, one_block, 0)

    def multiply(cg, out, g, start, stop):
        for kv in range(2):
            total = None
            if stop - start == W_CHUNKS:
                total = jnp.dot(xflat[g], wbuf[cg, kv], preferred_element_type=jnp.float32)
            else:
                for k in range(blocks):
                    at = slice(k * half + start * chunk, k * half + stop * chunk)
                    product = jnp.dot(xflat[g, :, at], wbuf[cg, kv, at, :], preferred_element_type=jnp.float32)
                    total = product if total is None else total + product
            for th in range(2):
                piece = total[th * group_tokens : (th + 1) * group_tokens]
                if start > 0:
                    out[th, kv, tokens(g), :] += piece
                else:
                    out[th, kv, tokens(g), :] = piece

    def far_done(g):
        far_swap(g).wait_recv()
        both = far[f, :, tokens(g), :] + far_peer[:, tokens(g), :]
        far_out[:, tokens(g), :] = both.astype(jnp.bfloat16)
        far_back(g).start()

    def x_ready(g):
        landed(xbuf.at[t, nf, some_rows(g)], x_recv.at[t, g])
        x_arrived(mirror, g)
        x_arrived(pair_mirror, g)
        flatten(g)

    w_last(0, 0)
    w_last(1, 0)

    @pl.when(middle)
    def _():
        x_ready(0)
        multiply(1, far, 0, 0, W_EARLY)
        multiply(0, near, 0, 0, W_EARLY)

    for c in range(W_EARLY, W_CHUNKS - 1):
        w_step(0, c)

    @pl.when(jnp.logical_not(middle))
    def _():
        x_arrived(pair, 0)
        x_ready(0)
        multiply(1, far, 0, 0, W_EARLY)
        multiply(0, near, 0, 0, W_EARLY)

    w_last(1, 1)
    multiply(1, far, 0, W_EARLY, W_CHUNKS)
    far_swap(0).start()

    @pl.when(middle)
    def _():
        x_ready(1)
        multiply(1, far, 1, 0, W_CHUNKS)
        far_swap(1).start()

    far_done(0)
    w_step(0, W_CHUNKS - 1)

    @pl.when(jnp.logical_not(middle))
    def _():
        x_arrived(pair, 1)
        x_ready(1)
        multiply(1, far, 1, 0, W_CHUNKS)
        far_swap(1).start()

    @pl.when(middle)
    def _():
        far_done(1)

    multiply(0, near, 1, 0, W_EARLY)

    @pl.when(jnp.logical_not(middle))
    def _():
        far_done(1)

    w_last(0, 1)
    for g in range(GROUPS):
        multiply(0, near, g, W_EARLY, W_CHUNKS)
        near_swap(g).start()

    drain(peer_grad, grad_send.at[0])
    drain(xbuf.at[0, 0], x_send.at[0])
    drain(xbuf.at[pl.ds(0, 2)], x_send.at[1])

    @pl.when(middle)
    def _():
        drain(xbuf.at[pl.ds(0, 2)], x_send.at[2])
        drain(xstage, x_send.at[3])

    drain(wpair, pair_send.at[0])
    drain(wbuf.at[:, :, pl.ds(0, 3 * half), :], w_send.at[0])
    drain(far.at[0], far_send.at[0])
    for copy in outs:
        copy.wait()
    for g in range(GROUPS):
        near_swap(g).wait_recv()
    for g in range(GROUPS):
        far_back(g).wait_recv()
    fresh_out[...] = (near[f] + near_peer[...] + far_in[...].astype(jnp.float32)).astype(jnp.bfloat16)
    drain(near.at[0], near_send.at[0])
    drain(far_out, back_send.at[0])


def tail_kernel(
    query_ref, old_ref, mass_ref, fresh_ref, master_in, one_in, two_in,
    context, master_out, one_out, two_out, out_ref, sem,
):
    moves = [
        pltpu.make_async_copy(source.at[kv], target.at[kv], sem.at[2 * i + kv])
        for i, (source, target) in enumerate(((master_in, master_out), (one_in, one_out), (two_in, two_out)))
        for kv in range(2)
    ]
    for move in moves:
        move.start()
    row_count, step_count, features = out_ref.shape
    head = HD
    groups = fresh_ref.shape[2] // head
    per_group = features // head // groups
    tokens = TAIL_ROWS * step_count
    parts = row_count // TAIL_ROWS
    token = lax.broadcasted_iota(jnp.int32, (tokens, 1), 0)
    column = lax.broadcasted_iota(jnp.int32, (1, tokens), 1)
    valid = (column // step_count == token // step_count) & (column <= token)
    factor = head**-0.5 * LOG2E
    contract = (((1,), (1,)), ((), ()))
    writes = []
    for part in range(parts):
        here = slice(part * tokens, (part + 1) * tokens)
        mine = slice(part * TAIL_ROWS, (part + 1) * TAIL_ROWS)
        for group in range(groups):
            cols = slice(group * head, (group + 1) * head)
            where = part * groups + group
            scores = lax.dot_general(
                query_ref[where], fresh_ref[0, here, cols], contract, preferred_element_type=jnp.float32
            )
            scores = jnp.where(valid[None], scores.reshape(per_group, tokens, tokens), LOW)
            scores = scores.reshape(per_group * tokens, tokens)
            mass = mass_ref[where]
            top = jnp.maximum(mass, jnp.max(scores, axis=-1, keepdims=True))
            old_weight = jnp.exp2((mass - top) * factor)
            weights = jnp.exp2((scores - top[:, :tokens]) * factor)
            scale = 1.0 / (old_weight + jnp.sum(weights, axis=-1, keepdims=True))
            new = jnp.dot(weights.astype(jnp.bfloat16), fresh_ref[1, here, cols], preferred_element_type=jnp.float32)
            out = (old_weight * old_ref[where] + new) * scale
            for h in range(per_group):
                at = (group * per_group + h) * head
                piece = out[h * tokens : (h + 1) * tokens].reshape(TAIL_ROWS, step_count, head)
                out_ref[mine, :, at : at + head] = piece.astype(jnp.bfloat16)
        write = pltpu.make_async_copy(out_ref.at[mine], context.at[mine], sem.at[6 + part])
        write.start()
        writes.append(write)
    for write in writes + moves:
        write.wait()


def fused_device(n_rep, grad_parts, master_weight, moment_one, moment_two, layer_inputs, queries, kv_cache, lengths):
    row_count, step_count, features = layer_inputs.shape
    _, depth, width = master_weight.shape
    n_tp = n_rep
    tokens = row_count * step_count
    bf16, f32 = jnp.bfloat16, jnp.float32
    dma = pltpu.SemaphoreType.DMA
    state = jax.ShapeDtypeStruct(master_weight.shape, f32)
    any_spec = pl.BlockSpec(memory_space=pl.ANY)
    hbm_spec = pl.BlockSpec(memory_space=pltpu.HBM)
    in_place = [
        pltpu.with_memory_space_constraint(array, pltpu.HBM)
        for array in (lengths, grad_parts, master_weight, moment_one, moment_two, layer_inputs, kv_cache, queries)
    ]
    half = depth // 2
    vmem_spec = pl.BlockSpec(memory_space=pltpu.VMEM)
    parts = row_count // TAIL_ROWS
    groups = width // HD
    stacked = (parts * groups, queries.shape[2] // width * TAIL_ROWS * step_count, HD)
    fresh, query, old, mass, master, one, two = pl.pallas_call(
        learner_kernel,
        out_shape=(
            jax.ShapeDtypeStruct((2, tokens, width), bf16),
            jax.ShapeDtypeStruct(stacked, bf16),
            jax.ShapeDtypeStruct(stacked, f32),
            jax.ShapeDtypeStruct(stacked, f32),
            state,
            state,
            state,
        ),
        in_specs=[hbm_spec] * 8,
        out_specs=(vmem_spec,) * 4 + (any_spec,) * 3,
        scratch_shapes=[
            pltpu.VMEM((2, depth, width), bf16),
            pltpu.VMEM((2, depth, width), bf16),
            pltpu.VMEM((2, depth, width), f32),
            pltpu.VMEM((2, depth, width), f32),
            pltpu.VMEM((2, depth, width), f32),
            pltpu.VMEM((2, half, width), bf16),
            pltpu.VMEM((2, 2, n_rep * half, width), bf16),
            pltpu.VMEM((n_tp, 2, row_count, step_count, half), bf16),
            pltpu.VMEM((2, row_count // GROUPS, step_count, half), bf16),
            pltpu.VMEM((GROUPS, 2 * tokens // GROUPS, n_tp * half), bf16),
            pltpu.VMEM((2, 2, tokens, width), f32),
            pltpu.VMEM((2, tokens, width), f32),
            pltpu.VMEM((2, tokens, width), bf16),
            pltpu.VMEM((2, tokens, width), bf16),
            pltpu.VMEM((2, 2, tokens, width), f32),
            pltpu.VMEM((2, tokens, width), f32),
            pltpu.VMEM(kv_cache.shape, bf16),
            pltpu.VMEM(queries.shape, bf16),
            pltpu.SMEM(lengths.shape, jnp.int32),
            dma((4, 2)),
            dma((4,)),
            dma((3,)),
            dma((1,)),
            dma((2 * W_CHUNKS,)),
            dma((4,)),
            dma((n_tp, GROUPS)),
            dma((1,)),
            dma((1,)),
            dma((W_CHUNKS,)),
            dma((1,)),
            dma((2, W_CHUNKS)),
            dma((2, 2)),
            dma((1,)),
            dma((GROUPS,)),
            dma((1,)),
            dma((GROUPS,)),
            dma((1,)),
            dma((GROUPS,)),
            pltpu.SemaphoreType.REGULAR((2,)),
        ],
        compiler_params=pltpu.CompilerParams(
            collective_id=0, has_side_effects=True, vmem_limit_bytes=36 * 1024 * 1024
        ),
    )(*in_place)
    context, master, one, two = pl.pallas_call(
        tail_kernel,
        out_shape=(jax.ShapeDtypeStruct(queries.shape, bf16), state, state, state),
        in_specs=[vmem_spec] * 4 + [any_spec] * 3,
        out_specs=(hbm_spec,) * 4,
        scratch_shapes=[pltpu.VMEM(queries.shape, bf16), dma((6 + parts,))],
        compiler_params=pltpu.CompilerParams(vmem_limit_bytes=16 * 1024 * 1024),
    )(query, old, mass, fresh, master, one, two)
    return (master, one, two, context)


beta_one = 0.9
beta_two = 0.95
learning_rate = 0.001
weight_decay = 0.1
epsilon = 1e-08
first_bias = 1.0 - 0.9**10
second_bias = 1.0 - 0.95**10


def adamw_update(gradient, master, moment_one, moment_two):
    new_one = beta_one * moment_one + (1.0 - beta_one) * gradient
    new_two = beta_two * moment_two + (1.0 - beta_two) * gradient * gradient
    update = new_one / first_bias / (jnp.sqrt(new_two / second_bias) + epsilon)
    new_master = master - learning_rate * (update + weight_decay * master)
    return (new_one, new_two, new_master)


def attend(queries, kv_cache, fresh_keys, fresh_values, lengths):
    row_count = queries.shape[0]
    step_count = queries.shape[1]
    kv_heads = fresh_keys.shape[2]
    cache_len = kv_cache.shape[1]
    grouped = queries.reshape(row_count, step_count, kv_heads, -1, HD)
    cached_keys = kv_cache[:, :, 0].reshape(row_count, cache_len, kv_heads, HD)
    cached_values = kv_cache[:, :, 1].reshape(row_count, cache_len, kv_heads, HD)
    scaling = 1.0 / jnp.sqrt(jnp.float32(HD))
    cached_scores = (
        jnp.einsum("rsgqd,rcgd->rsgqc", grouped, cached_keys, preferred_element_type=jnp.float32)
        * scaling
    )
    fresh_scores = (
        jnp.einsum("rsgqd,rugd->rsgqu", grouped, fresh_keys, preferred_element_type=jnp.float32)
        * scaling
    )
    valid_old = jnp.arange(cache_len, dtype=jnp.int32)[None, :] < lengths[:, None]
    valid_old = valid_old[:, None, None, None, :]
    steps_index = jnp.arange(step_count, dtype=jnp.int32)
    valid_new = (steps_index[None, :] <= steps_index[:, None])[None, :, None, None, :]
    scores = jnp.concatenate(
        [
            jnp.where(valid_old, cached_scores, -jnp.inf),
            jnp.where(valid_new, fresh_scores, -jnp.inf),
        ],
        axis=-1,
    )
    row_max = jnp.max(scores, axis=-1, keepdims=True)
    exponent = jnp.exp(scores - row_max)
    weights = (exponent / jnp.sum(exponent, axis=-1, keepdims=True)).astype(jnp.bfloat16)
    output = jnp.einsum(
        "rsgqc,rcgd->rsgqd",
        weights[..., :cache_len],
        cached_values,
        preferred_element_type=jnp.float32,
    )
    output = output + jnp.einsum(
        "rsgqu,rugd->rsgqd",
        weights[..., cache_len:],
        fresh_values,
        preferred_element_type=jnp.float32,
    )
    return output.astype(jnp.bfloat16).reshape(row_count, step_count, -1)


def on_device(
    grad_parts, master_weight, moment_one, moment_two, layer_inputs, queries, kv_cache, lengths
):
    gradient = lax.psum_scatter(
        grad_parts[0].astype(jnp.float32).astype(jnp.bfloat16),
        "fsdp",
        scatter_dimension=1,
        tiled=True,
    ).astype(jnp.float32)
    new_one, new_two, new_master = adamw_update(gradient, master_weight, moment_one, moment_two)
    rollout_weight = new_master.astype(jnp.bfloat16)
    row_count = layer_inputs.shape[0]
    step_count = layer_inputs.shape[1]
    gathered = lax.all_gather(layer_inputs, "tp", axis=2, tiled=True)
    flattened = gathered.reshape(row_count * step_count, gathered.shape[2])
    projected = jnp.einsum(
        "td,kdc->ktc",
        flattened,
        lax.all_gather(rollout_weight, ("rep", "fsdp"), axis=1, tiled=True),
        preferred_element_type=jnp.float32,
    )
    fresh_pair = projected.astype(jnp.bfloat16).reshape(2, row_count, step_count, -1, HD)
    context = attend(queries, kv_cache, fresh_pair[0], fresh_pair[1], lengths)
    return (new_master, new_one, new_two, context)


def solution(mesh):
    shape = mesh.shape
    fits = shape["rep"] == 4 and shape["tp"] == 4 and shape["fsdp"] == 2
    run = functools.partial(fused_device, shape["rep"]) if fits else on_device
    return jax.shard_map(
        run,
        mesh=mesh,
        in_specs=(
            P("fsdp", None, "rep", "tp"),
            P(None, ("rep", "fsdp"), "tp"),
            P(None, ("rep", "fsdp"), "tp"),
            P(None, ("rep", "fsdp"), "tp"),
            P(("rep", "fsdp"), None, "tp"),
            P(("rep", "fsdp"), None, "tp"),
            P(("rep", "fsdp"), None, None, "tp"),
            P(("rep", "fsdp")),
        ),
        out_specs=(
            P(None, ("rep", "fsdp"), "tp"),
            P(None, ("rep", "fsdp"), "tp"),
            P(None, ("rep", "fsdp"), "tp"),
            P(("rep", "fsdp"), None, "tp"),
        ),
        check_vma=False,
    )
```
